32 devices in a mesh: groups: 2 (over y), rows: 4 (over z), zero: 4 (over x, core).
Axes of the slice: x: 2, y: 2, z: 4, core: 2. Of those that a mesh axis runs over, the one named last changes fastest.
Arguments:
- latents: bfloat16 [8, 320, 32, 128], P(('groups', 'zero'), None, 'rows'), parts along dimension 0, may hold values from -40 to 40
- time_shift: float32 [8, 320], P(('groups', 'zero')), parts along dimension 0, may hold values from -4 to 4
- conv_first: bfloat16 [320, 9, 320], P('zero'), may hold values from -0.109375 to 0.109375
- conv_second: bfloat16 [320, 9, 320], P('zero'), may hold values from -0.1875 to 0.1875
- norm_gains: float32 [2, 320], replicated, may hold values from 0.5 to 1.5
- norm_biases: float32 [2, 320], replicated, may hold values from -3 to 3
- grad_output: bfloat16 [8, 320, 32, 128], P(('groups', 'zero'), None, 'rows'), parts along dimension 0, may hold values from -40 to 40
Outputs:
- block_out: bfloat16 [8, 320, 32, 128], P(('groups', 'zero'), None, 'rows'), parts along dimension 0
- grad_input: bfloat16 [8, 320, 32, 128], P(('groups', 'zero'), None, 'rows'), parts along dimension 0
- grad_time: float32 [8, 320], P(('groups', 'zero')), parts along dimension 0
- grad_conv_first: float32 [640, 9, 320], P(('groups', 'zero')), parts along dimension 0
- grad_conv_second: float32 [640, 9, 320], P(('groups', 'zero')), parts along dimension 0
- grad_norms: float32 [8, 320], P('groups'), parts along dimension 0
The draws below stay inside these ranges and needn't reach their ends.
There are 2 independent parts, one for each index of `groups`. The reference program is written for one: setup_inputs(seed, part) draws one part's arguments, and reference() takes and returns one part's arrays. A program takes and returns all parts, laid end to end along the dimension named above; an argument that names none is the same for every part. Nothing has to cross between parts.
All inputs are finite; a program needn't handle non-finite values.
Results may differ from the reference program's by a relative error of at most 0.0056.
Values may be sent and summed in bfloat16 or wider, within the bound.
A program may use at most 128 MiB of HBM per device.

```python
import jax
import jax.numpy as jnp
from jax import lax

C = 320
NORM_GROUPS = 32
W = 128
H = 32
IMAGES = 4


def latent_field(key):
    base_key, row_key, col_key = jax.random.split(key, 3)
    positions = jnp.arange(H, dtype=jnp.float32)
    rising = jnp.exp(jnp.log(3.0) * (positions / max(H - 1, 1) - 0.5))
    row_scale = 10.0 ** (jax.random.uniform(row_key, (H,), jnp.float32) - 0.5)
    col_scale = 10.0 ** (0.5 * jax.random.uniform(col_key, (W,), jnp.float32) - 0.25)
    sampled = jnp.clip(jax.random.normal(base_key, (IMAGES, C, H, W), jnp.float32), -4.0, 4.0)
    result_field = sampled * (rising * row_scale)[:, None] * col_scale[None, :]
    return result_field.astype(jnp.bfloat16)


def draw_latents(key, part):
    return latent_field(jax.random.fold_in(key, 11))


def draw_grad_output(key, part):
    return latent_field(jax.random.fold_in(key, 23))


def shard_levels(rng, dims, pieces, least, high):
    def one(axis_at, shards_of):
        steps = jax.random.uniform(jax.random.fold_in(jax.random.fold_in(rng, 6), axis_at), (shards_of,), jnp.float32, least / len(pieces), high / len(pieces))
        return jnp.repeat(jnp.exp(steps), dims[axis_at] // shards_of).reshape((-1,) + (1,) * (len(dims) - axis_at - 1))

    factor_of = one(*pieces[0])
    for cut in pieces[1:]:
        factor_of = factor_of * one(*cut)
    return factor_of


def normal_values(own_key, shape, spread, bound, shards=(), kind=jnp.bfloat16):
    values = spread * jax.random.normal(own_key, shape, jnp.float32)
    if shards:
        values = values * shard_levels(own_key, shape, shards, -0.22, 0.18)
    return jnp.clip(values, -bound, bound).astype(kind)


def setup_inputs(seed: int = 0, part: int = 0) -> dict:
    key_of = jax.random.split(jax.random.key(seed), 8)
    part_keys = jax.random.split(jax.random.fold_in(key_of[7], part), 8)
    latents = draw_latents(jax.random.fold_in(jax.random.fold_in(key_of[7], part), 71), part)
    time_shift = normal_values(part_keys[1], (IMAGES, C), 1.0, 4.0, ((0, 4),), jnp.float32)
    conv_first = normal_values(key_of[2], (C, 9, C), (9 * C) ** -0.5, 0.109375, ((0, 4),))
    conv_second = normal_values(key_of[3], (C, 9, C), (3 * C) ** -0.5, 0.1875, ((0, 4),))
    norm_gains = jnp.clip(jax.random.uniform(key_of[4], (2, C), jnp.float32, 0.5, 1.5), 0.5, 1.5)
    norm_biases = normal_values(key_of[5], (2, C), 0.5, 3.0, (), jnp.float32)
    grad_output = draw_grad_output(jax.random.fold_in(jax.random.fold_in(key_of[7], part), 71), part)
    return {"latents": latents, "time_shift": time_shift, "conv_first": conv_first, "conv_second": conv_second, "norm_gains": norm_gains, "norm_biases": norm_biases, "grad_output": grad_output}


EPSILON = 1e-05

def shifted_stack(field, flipped):
    padded = jnp.pad(field, ((0, 0), (1, 1), (1, 1)))
    slices = [padded[:, tap_row:tap_row + H, tap_col:tap_col + W] for tap_row in range(3) for tap_col in range(3)]
    if flipped:
        slices = slices[::-1]
    return jnp.stack(slices, axis=0).astype(jnp.float32)

def convolve(field, weights):
    return jnp.einsum('otc,tchw->ohw', weights.astype(jnp.float32), shifted_stack(field, False))

def convolve_back(field, weights):
    return jnp.einsum('otc,tohw->chw', weights.astype(jnp.float32), shifted_stack(field, True))

def weight_grad(cotangent, field):
    return jnp.einsum('ohw,tchw->otc', cotangent.astype(jnp.float32), shifted_stack(field, False))

def group_norm(values):
    grouped = values.reshape(NORM_GROUPS, C // NORM_GROUPS, H, W)
    average = lax.optimization_barrier(jnp.mean(grouped, axis=(1, 2, 3), keepdims=True))
    centered = grouped - average
    variance = lax.optimization_barrier(jnp.mean(centered * centered, axis=(1, 2, 3), keepdims=True))
    scaling = lax.rsqrt(variance + EPSILON)
    return ((centered * scaling).reshape(C, H, W), scaling)

def norm_back(grad_normed, normed, scaling):
    members = C // NORM_GROUPS * H * W
    grouped_grad = grad_normed.reshape(NORM_GROUPS, C // NORM_GROUPS, H, W)
    grouped_norm = normed.reshape(NORM_GROUPS, C // NORM_GROUPS, H, W)
    group_sum = lax.optimization_barrier(jnp.sum(grouped_grad, axis=(1, 2, 3), keepdims=True))
    cross_sum = lax.optimization_barrier(jnp.sum(grouped_grad * grouped_norm, axis=(1, 2, 3), keepdims=True))
    result = scaling * (grouped_grad - group_sum / members - grouped_norm * cross_sum / members)
    return result.reshape(C, H, W)

def silu_slope(pre_values):
    logistic = jax.nn.sigmoid(pre_values)
    return logistic * (1.0 + pre_values * (1.0 - logistic))

def reference(latents, time_shift, conv_first, conv_second, norm_gains, norm_biases, grad_output):
    gain_first = norm_gains[0][:, None, None]
    gain_second = norm_gains[1][:, None, None]
    bias_first = norm_biases[0][:, None, None]
    bias_second = norm_biases[1][:, None, None]

    def one_image(carry, inputs):
        grad_first, grad_second, norm_terms = carry
        latent, shift_row, cotangent = inputs
        normed_first, scale_first = group_norm(latent.astype(jnp.float32))
        pre_first = gain_first * normed_first + bias_first
        act_first = jax.nn.silu(pre_first).astype(jnp.bfloat16)
        hidden = (convolve(act_first, conv_first) + shift_row[:, None, None]).astype(jnp.bfloat16)
        normed_second, scale_second = group_norm(hidden.astype(jnp.float32))
        pre_second = gain_second * normed_second + bias_second
        act_second = jax.nn.silu(pre_second).astype(jnp.bfloat16)
        block = (latent.astype(jnp.float32) + convolve(act_second, conv_second)).astype(jnp.bfloat16)
        grad_second = grad_second + weight_grad(cotangent, act_second)
        back_second = convolve_back(cotangent, conv_second)
        slope_second = back_second * silu_slope(pre_second)
        grad_hidden = norm_back(gain_second * slope_second, normed_second, scale_second)
        time_grad = lax.optimization_barrier(jnp.sum(grad_hidden, axis=(1, 2)))
        hidden_grad = grad_hidden.astype(jnp.bfloat16)
        grad_first = grad_first + weight_grad(hidden_grad, act_first)
        back_first = convolve_back(hidden_grad, conv_first)
        slope_first = back_first * silu_slope(pre_first)
        grad_latent = norm_back(gain_first * slope_first, normed_first, scale_first)
        grad_in = (cotangent.astype(jnp.float32) + grad_latent).astype(jnp.bfloat16)
        local_terms = jnp.stack([lax.optimization_barrier(jnp.sum(slope_first * normed_first, axis=(1, 2))), lax.optimization_barrier(jnp.sum(slope_first, axis=(1, 2))), lax.optimization_barrier(jnp.sum(slope_second * normed_second, axis=(1, 2))), lax.optimization_barrier(jnp.sum(slope_second, axis=(1, 2)))])
        return ((grad_first, grad_second, norm_terms + local_terms), (block, grad_in, time_grad))
    initial = (jnp.zeros((C, 9, C), jnp.float32), jnp.zeros((C, 9, C), jnp.float32), jnp.zeros((4, C), jnp.float32))
    finals, stacked = lax.scan(one_image, initial, (latents, time_shift, grad_output))
    grad_first, grad_second, grad_norms = finals
    block_out, grad_input, grad_time = stacked
    return (block_out, grad_input, grad_time, grad_first, grad_second, grad_norms)
```

```python
import jax
import jax.numpy as jnp
import numpy as np
from jax import lax
from jax.experimental import pallas as pl
from jax.experimental.pallas import tpu as pltpu
from jax.sharding import PartitionSpec as P

NORM_GROUPS = 32
EPSILON = 1e-05
LANES = 128
F32 = jnp.float32
BF16 = jnp.bfloat16
MESH = pl.DeviceIdType.MESH


def block_kernel(
    x, g, gains, biases, shift, w1s, w2s, pool, spread,
    out, gin, small, dw1, dw2,
    act_stack, mid_stack, cot_stack, wfull1, wfull2, wturn1, wturn2,
    normed1, normed2, back, hgrad, cols, stat, halo_out, halo_in,
    part, core_in, core_keep, x_in, own, chain_in, chain_out, flat, vectors, tiny, tiny_x,
    send, recv,
):
    channels, cells = x.shape
    height = cells // LANES
    taps, shard, _ = w1s.shape
    depth = taps * channels
    rows = lax.axis_size("rows")
    row = lax.axis_index("rows")
    zero = lax.axis_index("zero")
    group = lax.axis_index("groups")
    core = lax.rem(zero, 2)
    mate = zero + 1 - 2 * core
    over = lax.rem(zero + 2, 4)
    over_mate = lax.rem(mate + 2, 4)
    blocks = channels // shard
    members = float(channels // NORM_GROUPS * cells * rows)
    lane = lax.broadcasted_iota(jnp.int32, (shard, LANES), 1)
    wide = lax.broadcasted_iota(jnp.int32, (channels, LANES), 1)
    counter = [0]

    def number():
        counter[0] += 1
        return counter[0] - 1

    pending = []

    def remote(src, dst, target):
        i = number()
        copy = pltpu.make_async_remote_copy(
            src_ref=src, dst_ref=dst, send_sem=send.at[i], recv_sem=recv.at[i],
            device_id=target, device_id_type=MESH,
        )
        return copy

    def go(src, dst, target):
        copy = remote(src, dst, target)
        copy.start()
        pending.append(copy)
        return copy

    def to_rows(src, dst):
        return [go(src, dst, {"rows": lax.rem(row + d, rows)}) for d in range(1, rows)]

    def chunked(body):
        def step(c, _):
            body(pl.multiple_of(c * shard, shard))
            return 0
        lax.fori_loop(0, blocks, step, 0)

    def put(stack, value, start, p, flip):
        left = jnp.where(lane == 0, 0.0, pltpu.roll(value, 1, 1)).astype(BF16)
        right = jnp.where(lane == LANES - 1, 0.0, pltpu.roll(value, LANES - 1, 1)).astype(BF16)
        slabs = (left, value.astype(BF16), right)
        for ty in range(3):
            h = p - 2 + ty if flip else p - ty
            if 0 <= h < height:
                for tx in range(3):
                    tap = 3 * ty + tx
                    stack[pl.ds(start + tap * channels, shard), h * LANES : (h + 1) * LANES] = (
                        slabs[2 - tx if flip else tx]
                    )

    def line(h):
        return slice(h * LANES, (h + 1) * LANES)

    def halo_start(stage, top, bottom):
        down = remote(bottom, halo_in.at[stage, 0], {"rows": lax.rem(row + 1, rows)})
        up = remote(top, halo_in.at[stage, 1], {"rows": lax.rem(row + rows - 1, rows)})

        @pl.when(row < rows - 1)
        def _():
            down.start()

        @pl.when(row > 0)
        def _():
            up.start()

        return down, up

    def halo_finish(stage, pair, stack, flip, turned=None):
        down, up = pair

        @pl.when(row > 0)
        def _():
            down.wait_recv()
            up.wait_send()

        @pl.when(row < rows - 1)
        def _():
            up.wait_recv()
            down.wait_send()

        @pl.when(row == 0)
        def _():
            halo_in[stage, 0] = jnp.zeros((channels, LANES), BF16)

        @pl.when(row == rows - 1)
        def _():
            halo_in[stage, 1] = jnp.zeros((channels, LANES), BF16)

        def body(start):
            for side, p, inside in ((0, 0, row > 0), (1, height + 1, row < rows - 1)):
                value = halo_in[stage, side, pl.ds(start, shard), :].astype(F32)
                if turned is not None:
                    value = jnp.where(inside, turned(pl.ds(start, shard), value), 0.0)
                put(stack, value, start, p, flip)
        chunked(body)

    def lane_sum(value):
        return jnp.sum(value, axis=1, keepdims=True)

    def stat_start(stage, first, second):
        packed = jnp.where(wide == 0, first, jnp.where(wide == 1, second, 0.0))
        stat[stage, row] = jnp.dot(
            pool[...], packed, precision=lax.Precision.HIGHEST, preferred_element_type=F32
        )
        return to_rows(stat.at[stage, row], stat.at[stage, row])

    def stat_finish(stage, copies):
        for copy in copies:
            copy.wait_recv()
        total = stat[stage, 0]
        for i in range(1, rows):
            total = total + stat[stage, i]
        wide_total = jnp.dot(
            spread[...], total, precision=lax.Precision.HIGHEST, preferred_element_type=F32
        ) / members
        return wide_total[:, 0:1], wide_total[:, 1:2]

    def column(i, value):
        cols[i] = jnp.broadcast_to(value, (channels, LANES))

    def moments(stage, copies, at):
        average, square = stat_finish(stage, copies)
        column(at, average)
        column(at + 1, lax.rsqrt(square - average * average + EPSILON))

    barrier = pltpu.get_barrier_semaphore()
    for d in range(1, rows):
        pl.semaphore_signal(
            barrier, inc=1, device_id={"rows": lax.rem(row + d, rows)}, device_id_type=MESH
        )
    for target in ({"zero": mate}, {"zero": over}, {"groups": 1 - group}):
        pl.semaphore_signal(barrier, inc=1, device_id=target, device_id_type=MESH)

    vectors[...] = jnp.zeros_like(vectors)
    vectors[0:2, 0:channels] = gains[...]
    vectors[2:4, 0:channels] = biases[...]
    vectors[4:5, 0:channels] = shift[...]
    pv = vectors[...].T[:channels, :]
    GAIN1, GAIN2 = pv[:, 0:1], pv[:, 1:2]
    SUM_A, SUM_B, SUM_C, SUM_D, SUM_T = 13, 14, 15, 16, 17
    for i in range(5):
        column((8, 10, 9, 11, 12)[i], pv[:, i : i + 1])

    def first_sums(start):
        total = jnp.zeros((shard, LANES), F32)
        square = total
        for h in range(height):
            value = x[pl.ds(start, shard), line(h)].astype(F32)
            total = total + value
            square = square + value * value
        cols[SUM_A, pl.ds(start, shard), :] = total
        cols[SUM_B, pl.ds(start, shard), :] = square
    chunked(first_sums)
    s0, s1 = lane_sum(cols[SUM_A]), lane_sum(cols[SUM_B])

    pl.semaphore_wait(barrier, rows - 1 + 3)
    stat0 = stat_start(0, s0, s1)
    halo_a = halo_start(1, x.at[:, 0:LANES], x.at[:, (height - 1) * LANES : height * LANES])
    halo_g = halo_start(0, g.at[:, 0:LANES], g.at[:, (height - 1) * LANES : height * LANES])

    def flatten(own, full):
        full[zero] = jnp.concatenate([own[tap] for tap in range(taps)], axis=1)

    SLICE = 16
    COMMON = (shard // SLICE - 1) // 2 * SLICE

    def gather_start(full):
        mine = full.at[zero]
        near = go(mine, mine, {"zero": mate})
        far = []
        for i in range(COMMON // SLICE):
            at = pl.ds(pl.multiple_of(group * COMMON + i * SLICE, SLICE), SLICE)
            far.append(go(mine.at[at], mine.at[at], {"zero": over}))
        at = pl.ds(2 * COMMON, shard - 2 * COMMON)
        far.append(go(mine.at[at], mine.at[at], {"zero": over}))
        return near, far

    def gather_pass(full, far):
        theirs = full.at[over]
        passed, crossed = [], []
        for i in range(COMMON // SLICE):
            at = pl.ds(pl.multiple_of(group * COMMON + i * SLICE, SLICE), SLICE)
            far[i].wait_recv()
            crossed.append(go(theirs.at[at], theirs.at[at], {"groups": 1 - group}))
            passed.append(go(theirs.at[at], theirs.at[at], {"zero": mate}))
        return passed, crossed

    def gather_rest(full, far, passed, crossed):
        theirs = full.at[over]
        far[-1].wait_recv()
        at = pl.ds(2 * COMMON, shard - 2 * COMMON)
        passed.append(go(theirs.at[at], theirs.at[at], {"zero": mate}))
        for i in range(COMMON // SLICE):
            at = pl.ds(pl.multiple_of((1 - group) * COMMON + i * SLICE, SLICE), SLICE)
            crossed[i].wait_recv()
            passed.append(go(theirs.at[at], theirs.at[at], {"zero": mate}))

    def gather_finish(near, passed):
        near.wait_recv()
        for copy in passed:
            copy.wait_recv()

    flatten(w1s, wfull1)
    near1, far1 = gather_start(wfull1)
    flatten(w2s, wfull2)

    moments(0, stat0, 0)

    def first_act(start):
        at = pl.ds(start, shard)
        for h in range(height):
            normed = (x[at, line(h)].astype(F32) - cols[0, at, :]) * cols[1, at, :]
            normed1[at, line(h)] = normed
            pre = cols[8, at, :] * normed + cols[9, at, :]
            act = (pre / (1.0 + jnp.exp(-pre))).astype(BF16).astype(F32)
            put(act_stack, act, start, h + 1, False)
    chunked(first_act)

    def first_edge(at, value):
        pre = cols[8, at, :] * ((value - cols[0, at, :]) * cols[1, at, :]) + cols[9, at, :]
        return (pre / (1.0 + jnp.exp(-pre))).astype(BF16).astype(F32)
    halo_finish(1, halo_a, act_stack, False, first_edge)
    passed1, crossed1 = gather_pass(wfull1, far1)
    near2, far2 = gather_start(wfull2)

    def cot_fill(start):
        for h in range(height):
            put(cot_stack, g[pl.ds(start, shard), line(h)].astype(F32), start, h + 1, True)
    chunked(cot_fill)
    halo_finish(0, halo_g, cot_stack, True)
    gather_rest(wfull1, far1, passed1, crossed1)
    passed2, crossed2 = gather_pass(wfull2, far2)
    gather_finish(near1, passed1)

    TILE = 256

    count = cells // TILE

    def tiles(body, first=0, last=count):
        def step(i, _):
            body(pl.ds(pl.multiple_of(i * TILE, TILE), TILE))
            return 0
        lax.fori_loop(first, last, step, 0)

    def conv(full, stack, emit, first=0, last=count):
        def tile(at):
            weights = full[...].reshape(channels, full.shape[2])
            emit(at, jnp.dot(weights, stack[:, at], preferred_element_type=F32))
        tiles(tile, first, last)

    def emit_hidden(at, value):
        shift = cols[12][:, 0:1]
        normed2[:, at] = (value + shift).astype(BF16).astype(F32)
    conv(wfull1, act_stack, emit_hidden)

    def second_sums(start):
        total = jnp.zeros((shard, LANES), F32)
        square = total
        for h in range(height):
            value = normed2[pl.ds(start, shard), line(h)]
            total = total + value
            square = square + value * value
            if h == 0:
                halo_out[0, 0, pl.ds(start, shard), :] = value.astype(BF16)
            if h == height - 1:
                halo_out[0, 1, pl.ds(start, shard), :] = value.astype(BF16)
        cols[SUM_A, pl.ds(start, shard), :] = total
        cols[SUM_B, pl.ds(start, shard), :] = square
    chunked(second_sums)
    stat1 = stat_start(1, lane_sum(cols[SUM_A]), lane_sum(cols[SUM_B]))
    halo_b = halo_start(2, halo_out.at[0, 0], halo_out.at[0, 1])

    PAIR = 2 * channels

    def turn(full, wturn):
        for begin in range(0, depth, PAIR):
            end = min(begin + PAIR, depth)
            weights = full[:, :, begin:end].reshape(channels, end - begin)
            turned = weights.T
            wturn[:, begin:end] = jnp.concatenate(
                [turned[i : i + channels] for i in range(0, end - begin, channels)], axis=1
            )

    def conv_back(stack, wturn):
        def tile(at):
            total = jnp.dot(wturn[...], stack[:, at], preferred_element_type=F32)
            back[:, at] = total
        tiles(tile)

    gather_rest(wfull2, far2, passed2, crossed2)
    turn(wfull1, wturn1)
    gather_finish(near2, passed2)
    turn(wfull2, wturn2)
    conv_back(cot_stack, wturn2)
    moments(1, stat1, 2)

    def second_act(start):
        at = pl.ds(start, shard)
        sums = [jnp.zeros((shard, LANES), F32)] * 2
        for h in range(height):
            normed = (normed2[at, line(h)] - cols[2, at, :]) * cols[3, at, :]
            normed2[at, line(h)] = normed
            pre = cols[10, at, :] * normed + cols[11, at, :]
            q = 1.0 / (1.0 + jnp.exp(-pre))
            act = (pre * q).astype(BF16).astype(F32)
            slope = back[at, line(h)] * (q * (1.0 + pre * (1.0 - q)))
            back[at, line(h)] = slope
            sums = [sums[0] + slope * normed, sums[1] + slope]
            put(mid_stack, act, start, h + 1, False)
        cols[SUM_C, at, :] = sums[0]
        cols[SUM_D, at, :] = sums[1]
    chunked(second_act)
    gain_cross2, bias_sum2 = lane_sum(cols[SUM_C]), lane_sum(cols[SUM_D])
    stat2 = stat_start(2, GAIN2 * bias_sum2, GAIN2 * gain_cross2)

    def second_edge(at, value):
        pre = cols[10, at, :] * ((value - cols[2, at, :]) * cols[3, at, :]) + cols[11, at, :]
        return (pre * (1.0 / (1.0 + jnp.exp(-pre)))).astype(BF16).astype(F32)
    halo_finish(2, halo_b, mid_stack, False, second_edge)

    total_width = part.shape[3]
    last_row = rows - 1
    nearer = jnp.where(row < rows // 2, 0, 1)

    def weight_grad(stream, cot, stack):
        which, first, last = stream
        value = lax.dot_general(
            cot[...], stack[first:last, :], (((1,), (1,)), ((), ())), preferred_element_type=F32
        )
        part[which, :, :, first:last] = value.astype(BF16).reshape(blocks, shard, last - first)
        at = extent(stream)
        return [
            go(part.at[which, over_mate, :, at], core_in.at[which, 1, :, at], {"zero": mate}),
            go(part.at[which, mate, :, at], core_in.at[which, 0, :, at], {"zero": mate}),
        ]

    def extent(stream):
        _, first, last = stream
        return slice(first, -(-last // LANES) * LANES)

    def reduce_core(stream, copies):
        which, at = stream[0], extent(stream)
        copies[0].wait_recv()
        core_keep[which, :, at] = (
            part[which, over, :, at].astype(F32) + core_in[which, 1, :, at].astype(F32)
        ).astype(BF16)
        return copies[1], go(core_keep.at[which, :, at], x_in.at[which, :, at], {"zero": over})

    def reduce_over(stream, copies):
        which, at = stream[0], extent(stream)
        for copy in copies:
            copy.wait_recv()
        value = (
            part[which, zero, :, at].astype(F32)
            + core_in[which, 0, :, at].astype(F32)
            + x_in[which, :, at].astype(F32)
        )
        own[which, :, at] = value.astype(BF16)
        i = number()
        number()
        links = []
        for way in (nearer, 1 - nearer):
            links.append(pltpu.make_async_remote_copy(
                src_ref=chain_out.at[way, which, :, at],
                dst_ref=chain_in.at[way, which, :, at],
                send_sem=send.at[i + way], recv_sem=recv.at[i + way],
                device_id={"rows": jnp.clip(row + 1 - 2 * way, 0, last_row)}, device_id_type=MESH,
            ))
        arrives = [jnp.where(way == 0, row > 0, row < last_row) for way in (nearer, 1 - nearer)]
        leaves = [jnp.where(way == 0, row < last_row, row > 0) for way in (nearer, 1 - nearer)]
        for k, way in enumerate((nearer, 1 - nearer)):
            @pl.when(leaves[k] & jnp.logical_not(arrives[k]))
            def _(k=k, way=way):
                chain_out[way, which, :, at] = value.astype(chain_out.dtype)
                links[k].start()
        return links, arrives, leaves

    def chain_step(stream, state, k):
        which, at = stream[0], extent(stream)
        links, arrives, leaves = state
        way = (nearer, 1 - nearer)[k]

        @pl.when(leaves[k] & arrives[k])
        def _():
            links[k].wait_recv()
            chain_out[way, which, :, at] = (
                chain_in[way, which, :, at].astype(F32) + own[which, :, at].astype(F32)
            ).astype(chain_out.dtype)
            links[k].start()
        return state

    def chain_finish(stream, state):
        which, at = stream[0], extent(stream)
        links, arrives, leaves = state
        flat[which, :, at] = own[which, :, at].astype(F32)
        for k, way in enumerate((nearer, 1 - nearer)):
            @pl.when(arrives[k])
            def _(k=k, way=way):
                @pl.when(jnp.logical_not(leaves[k]))
                def _():
                    links[k].wait_recv()
                flat[which, :, at] += chain_in[way, which, :, at].astype(F32)

            @pl.when(leaves[k])
            def _(k=k):
                links[k].wait_send()

    def reduce_finish(which, target):
        for tap in range(taps):
            target[tap] = flat[which, :, tap * channels : (tap + 1) * channels]

    WIDTH = 6 * LANES
    second = [(1, first, min(first + WIDTH, depth)) for first in range(0, depth, WIDTH)]
    first = [(0, first, min(first + WIDTH, depth)) for first in range(0, depth, WIDTH)]
    streams = second + first
    state = {}

    def grad(k, cot, stack):
        state[k] = weight_grad(streams[k], cot, stack)

    def core_step(k):
        state[k] = reduce_core(streams[k], state[k])

    def over_step(k):
        state[k] = reduce_over(streams[k], state[k])

    def near_step(k):
        state[k] = chain_step(streams[k], state[k], 0)

    def far_step(k):
        state[k] = chain_step(streams[k], state[k], 1)

    def end_step(k):
        chain_finish(streams[k], state[k])

    grad(0, g, mid_stack)
    grad(1, g, mid_stack)
    core_step(0)
    grad(2, g, mid_stack)
    core_step(1)
    grad(3, g, mid_stack)
    core_step(2)

    average, cross = stat_finish(2, stat2)
    column(4, average)
    column(5, cross)
    core_step(3)

    def hidden_back(start):
        at = pl.ds(start, shard)
        total = jnp.zeros((shard, LANES), F32)
        for h in range(height):
            value = cols[3, at, :] * (
                cols[10, at, :] * back[at, line(h)]
                - cols[4, at, :]
                - normed2[at, line(h)] * cols[5, at, :]
            )
            total = total + value
            rounded = value.astype(BF16)
            hgrad[at, line(h)] = rounded
            put(cot_stack, rounded.astype(F32), start, h + 1, True)
            if h == 0:
                halo_out[2, 0, at, :] = rounded
            if h == height - 1:
                halo_out[2, 1, at, :] = rounded
        cols[SUM_T, at, :] = total
    chunked(hidden_back)
    halo_h = halo_start(3, halo_out.at[2, 0], halo_out.at[2, 1])
    time_sum = lane_sum(cols[SUM_T])

    over_step(0)
    grad(4, hgrad, act_stack)
    grad(5, hgrad, act_stack)
    core_step(4)
    grad(6, hgrad, act_stack)
    core_step(5)
    grad(7, hgrad, act_stack)
    core_step(6)
    over_step(1)
    core_step(7)
    near_step(0)
    halo_finish(3, halo_h, cot_stack, True)
    conv_back(cot_stack, wturn1)
    over_step(2)
    near_step(1)
    over_step(3)
    far_step(0)

    def first_slope(start):
        at = pl.ds(start, shard)
        sums = [jnp.zeros((shard, LANES), F32)] * 2
        for h in range(height):
            normed = normed1[at, line(h)]
            pre = cols[8, at, :] * normed + cols[9, at, :]
            q = 1.0 / (1.0 + jnp.exp(-pre))
            slope = back[at, line(h)] * (q * (1.0 + pre * (1.0 - q)))
            back[at, line(h)] = slope
            sums = [sums[0] + slope * normed, sums[1] + slope]
        cols[SUM_A, at, :] = sums[0]
        cols[SUM_B, at, :] = sums[1]
    chunked(first_slope)
    gain_cross1, bias_sum1 = lane_sum(cols[SUM_A]), lane_sum(cols[SUM_B])
    stat3 = stat_start(3, GAIN1 * bias_sum1, GAIN1 * gain_cross1)
    near_step(2)
    over_step(4)
    far_step(1)
    packed = jnp.zeros((channels, LANES), F32)
    for i, value in enumerate((time_sum, gain_cross1, bias_sum1, gain_cross2, bias_sum2)):
        packed = jnp.where(wide == i, value, packed)
    fill = jnp.zeros((tiny.shape[2] - channels, LANES), F32)
    tiny[row] = jnp.concatenate([packed, fill], axis=0).T[:8, :]
    tiny_rows = to_rows(tiny.at[row], tiny.at[row])

    def emit_out(at, value):
        out[:, at] = (x[:, at].astype(F32) + value).astype(BF16)
    conv(wfull2, mid_stack, emit_out, 0, count // 2)
    near_step(3)
    over_step(5)
    far_step(2)
    end_step(0)
    conv(wfull2, mid_stack, emit_out, count // 2, count)
    near_step(4)
    over_step(6)
    far_step(3)
    end_step(1)

    average, cross = stat_finish(3, stat3)
    column(6, average)
    column(7, cross)

    for copy in tiny_rows:
        copy.wait_recv()
    total = tiny[0]
    for i in range(1, rows):
        total = total + tiny[i]
    tiny_x[0] = total
    first_hop = go(tiny_x.at[0], tiny_x.at[1], {"zero": mate})
    def input_back(start):
        at = pl.ds(start, shard)
        for h in range(height):
            value = cols[1, at, :] * (
                cols[8, at, :] * back[at, line(h)]
                - cols[6, at, :]
                - normed1[at, line(h)] * cols[7, at, :]
            )
            gin[at, line(h)] = (g[at, line(h)].astype(F32) + value).astype(BF16)
    chunked(input_back)

    first_hop.wait_recv()
    tiny_x[2] = total + tiny_x[1]
    second_hop = go(tiny_x.at[2], tiny_x.at[3], {"zero": over})
    near_step(5)
    over_step(7)
    far_step(4)
    end_step(2)
    near_step(6)
    end_step(3)
    reduce_finish(1, dw2)
    second_hop.wait_recv()
    pick = lax.broadcasted_iota(jnp.int32, total.shape, 0)
    small[...] = jnp.where(pick == 0, total, tiny_x[2] + tiny_x[3])
    far_step(5)
    near_step(7)
    end_step(4)
    far_step(6)
    end_step(5)
    far_step(7)
    end_step(6)
    end_step(7)
    reduce_finish(0, dw1)
    for copy in pending:
        copy.wait_send()


def local(latents, time_shift, conv_first, conv_second, norm_gains, norm_biases, grad_output):
    _, channels, height, width = latents.shape
    cells = height * width
    shard, taps, _ = conv_first.shape
    depth = taps * channels
    rows = lax.axis_size("rows")
    blocks = channels // shard
    group = np.arange(channels) // (channels // NORM_GROUPS)
    pool = (group[None, :] == np.arange(NORM_GROUPS)[:, None]).astype(np.float32)
    span = -(-depth // LANES) * LANES
    chain = BF16 if rows <= 8 else F32
    padded = -(-channels // LANES) * LANES
    vmem = pl.BlockSpec(memory_space=pltpu.VMEM)
    copies = 5 * (rows - 1) + 8 + 2 * 12 + 8 * 5 + 2
    field = jax.ShapeDtypeStruct((channels, cells), BF16)
    grads = jax.ShapeDtypeStruct((taps, shard, channels), F32)
    out, gin, small, dw1, dw2 = pl.pallas_call(
        block_kernel,
        out_shape=(field, field, jax.ShapeDtypeStruct((8, padded), F32), grads, grads),
        in_specs=[vmem] * 9,
        out_specs=(vmem,) * 5,
        scratch_shapes=[
            pltpu.VMEM((depth, cells), BF16),
            pltpu.VMEM((depth, cells), BF16),
            pltpu.VMEM((depth, cells), BF16),
            pltpu.VMEM((blocks, shard, depth), BF16),
            pltpu.VMEM((blocks, shard, depth), BF16),
            pltpu.VMEM((channels, depth), BF16),
            pltpu.VMEM((channels, depth), BF16),
            pltpu.VMEM((channels, cells), F32),
            pltpu.VMEM((channels, cells), F32),
            pltpu.VMEM((channels, cells), F32),
            pltpu.VMEM((channels, cells), BF16),
            pltpu.VMEM((18, channels, LANES), F32),
            pltpu.VMEM((4, rows, NORM_GROUPS, LANES), F32),
            pltpu.VMEM((3, 2, channels, LANES), BF16),
            pltpu.VMEM((4, 2, channels, LANES), BF16),
            pltpu.VMEM((2, blocks, shard, span), BF16),
            pltpu.VMEM((2, 2, shard, span), BF16),
            pltpu.VMEM((2, shard, span), BF16),
            pltpu.VMEM((2, shard, span), BF16),
            pltpu.VMEM((2, shard, span), BF16),
            pltpu.VMEM((2, 2, shard, span), chain),
            pltpu.VMEM((2, 2, shard, span), chain),
            pltpu.VMEM((2, shard, span), F32),
            pltpu.VMEM((LANES, padded), F32),
            pltpu.VMEM((rows, 8, padded), F32),
            pltpu.VMEM((4, 8, padded), F32),
            pltpu.SemaphoreType.DMA((copies,)),
            pltpu.SemaphoreType.DMA((copies,)),
        ],
        compiler_params=pltpu.CompilerParams(
            collective_id=0, has_side_effects=True, vmem_limit_bytes=60 * 1024 * 1024
        ),
    )(
        latents.reshape(channels, cells),
        grad_output.reshape(channels, cells),
        norm_gains,
        norm_biases,
        time_shift,
        jnp.transpose(conv_first, (1, 0, 2)),
        jnp.transpose(conv_second, (1, 0, 2)),
        jnp.asarray(pool),
        jnp.asarray(np.ascontiguousarray(pool.T)),
    )
    return (
        out.reshape(latents.shape),
        gin.reshape(latents.shape),
        small[0:1, :channels],
        jnp.transpose(dw1, (1, 0, 2)),
        jnp.transpose(dw2, (1, 0, 2)),
        small[1:5, :channels],
    )


def solution(mesh):
    placed = (
        P(("groups", "zero"), None, "rows", None),
        P(("groups", "zero"), None),
        P("zero", None, None),
        P("zero", None, None),
        P(),
        P(),
        P(("groups", "zero"), None, "rows", None),
    )
    return jax.shard_map(
        local,
        mesh=mesh,
        in_specs=placed,
        out_specs=(
            P(("groups", "zero"), None, "rows", None),
            P(("groups", "zero"), None, "rows", None),
            P(("groups", "zero"), None),
            P(("groups", "zero"), None, None),
            P(("groups", "zero"), None, None),
            P("groups", None),
        ),
        check_vma=False,
    )
```

```python
import jax
import jax.numpy as jnp
import numpy as np
from jax import lax
from jax.experimental import pallas as pl
from jax.experimental.pallas import tpu as pltpu
from jax.sharding import PartitionSpec as P

NORM_GROUPS = 32
EPSILON = 1e-05
LANES = 128
F32 = jnp.float32
BF16 = jnp.bfloat16
MESH = pl.DeviceIdType.MESH


def block_kernel(
    x, g, gains, biases, shift, w1s, w2s, pool, spread,
    out, gin, small, dw1, dw2,
    act_slab, mid_slab, cot_slab, wfull1, wfull2, wturn1, wturn2,
    xs, gs, hidden, normed1, normed2, back, hgrad, lines, cols, stat, halo_in,
    part, core_in, core_keep, x_in, own, chain_in, chain_out, flat,
    out_stage, gin_stage, dw_stage, vectors, tiny, tiny_x,
    send, recv, local_sem,
):
    channels, height, _ = x.shape
    cells = height * LANES
    taps, shard, _ = w1s.shape
    bands = taps // 3
    used = bands * channels
    band = wturn1.shape[1] // 3
    rows = lax.axis_size("rows")
    row = lax.axis_index("rows")
    zero = lax.axis_index("zero")
    group = lax.axis_index("groups")
    core = lax.rem(zero, 2)
    mate = zero + 1 - 2 * core
    over = lax.rem(zero + 2, 4)
    over_mate = lax.rem(mate + 2, 4)
    blocks = channels // shard
    members = float(channels // NORM_GROUPS * cells * rows)
    lane = lax.broadcasted_iota(jnp.int32, (shard, LANES), 1)
    wide = lax.broadcasted_iota(jnp.int32, (channels, LANES), 1)
    counter = [0]
    local_counter = [0]

    def number():
        counter[0] += 1
        return counter[0] - 1

    pending = []
    stores = []

    def store_out(src, dst):
        i = local_counter[0]
        local_counter[0] += 1
        copy = pltpu.make_async_copy(src, dst, local_sem.at[i])
        copy.start()
        stores.append(copy)

    def remote(src, dst, target):
        i = number()
        return pltpu.make_async_remote_copy(
            src_ref=src, dst_ref=dst, send_sem=send.at[i], recv_sem=recv.at[i],
            device_id=target, device_id_type=MESH,
        )

    def go(src, dst, target):
        copy = remote(src, dst, target)
        copy.start()
        pending.append(copy)
        return copy

    def to_rows(src, dst):
        return [go(src, dst, {"rows": lax.rem(row + d, rows)}) for d in range(1, rows)]

    def chunked(body):
        def step(c, _):
            body(pl.multiple_of(c * shard, shard))
            return 0
        lax.fori_loop(0, blocks, step, 0)

    def put(slab, value, start, p):
        left = jnp.where(lane == 0, 0.0, pltpu.roll(value, 1, 1)).astype(BF16)
        right = jnp.where(lane == LANES - 1, 0.0, pltpu.roll(value, LANES - 1, 1)).astype(BF16)
        for tx, shifted in enumerate((left, value.astype(BF16), right)):
            slab[pl.ds(start + tx * channels, shard), p * LANES : (p + 1) * LANES] = shifted

    def line(h):
        return slice(h * LANES, (h + 1) * LANES)

    def spread_lines(field, start):
        at = pl.ds(pl.multiple_of(start * height, shard * height), shard * height)
        lines[at, :] = field[pl.ds(start, shard)].astype(F32).reshape(shard * height, LANES)

    def read_line(start, h):
        return lines[pl.ds(start * height + h, shard, stride=height), :]

    def write_line(start, h, value):
        lines[pl.ds(start * height + h, shard, stride=height), :] = value

    def collect_lines(stage, start):
        at = pl.ds(pl.multiple_of(start * height, shard * height), shard * height)
        stage[pl.ds(start, shard)] = lines[at, :].reshape(shard, height, LANES).astype(BF16)

    def halo_start(stage, top, bottom):
        down = remote(bottom, halo_in.at[stage, 0], {"rows": lax.rem(row + 1, rows)})
        up = remote(top, halo_in.at[stage, 1], {"rows": lax.rem(row + rows - 1, rows)})

        @pl.when(row < rows - 1)
        def _():
            down.start()

        @pl.when(row > 0)
        def _():
            up.start()

        return down, up

    def halo_edges(stage, field):
        return halo_start(stage, field.at[:, line(0)], field.at[:, line(height - 1)])

    def halo_finish(stage, pair, slab, turned=None):
        down, up = pair

        @pl.when(row > 0)
        def _():
            down.wait_recv()
            up.wait_send()

        @pl.when(row < rows - 1)
        def _():
            up.wait_recv()
            down.wait_send()

        @pl.when(row == 0)
        def _():
            halo_in[stage, 0] = jnp.zeros((channels, LANES), BF16)

        @pl.when(row == rows - 1)
        def _():
            halo_in[stage, 1] = jnp.zeros((channels, LANES), BF16)

        def body(start):
            for side, p, inside in ((0, 0, row > 0), (1, height + 1, row < rows - 1)):
                value = halo_in[stage, side, pl.ds(start, shard), :].astype(F32)
                if turned is not None:
                    value = jnp.where(inside, turned(pl.ds(start, shard), value), 0.0)
                put(slab, value, start, p)
        chunked(body)

    def lane_sum(value):
        return jnp.sum(value, axis=1, keepdims=True)

    def stat_start(stage, first, second):
        packed = jnp.where(wide == 0, first, jnp.where(wide == 1, second, 0.0))
        stat[stage, row] = jnp.dot(
            pool[...], packed, precision=lax.Precision.HIGHEST, preferred_element_type=F32
        )
        return to_rows(stat.at[stage, row], stat.at[stage, row])

    def stat_finish(stage, copies):
        for copy in copies:
            copy.wait_recv()
        total = stat[stage, 0]
        for i in range(1, rows):
            total = total + stat[stage, i]
        wide_total = jnp.dot(
            spread[...], total, precision=lax.Precision.HIGHEST, preferred_element_type=F32
        ) / members
        return wide_total[:, 0:1], wide_total[:, 1:2]

    def column(i, value):
        cols[i] = jnp.broadcast_to(value, (channels, LANES))

    def moments(stage, copies, at):
        average, square = stat_finish(stage, copies)
        column(at, average)
        column(at + 1, lax.rsqrt(square - average * average + EPSILON))

    barrier = pltpu.get_barrier_semaphore()
    for d in range(1, rows):
        pl.semaphore_signal(
            barrier, inc=1, device_id={"rows": lax.rem(row + d, rows)}, device_id_type=MESH
        )
    for target in ({"zero": mate}, {"zero": over}, {"groups": 1 - group}):
        pl.semaphore_signal(barrier, inc=1, device_id=target, device_id_type=MESH)

    def flatten(shards, full):
        for b in range(3):
            full[zero, :, b * band : b * band + used] = jnp.concatenate(
                [shards[bands * b + i] for i in range(bands)], axis=1
            )

    flatten(w1s, wfull1)
    vectors[...] = jnp.zeros_like(vectors)
    vectors[0:2, 0:channels] = gains[...]
    vectors[2:4, 0:channels] = biases[...]
    vectors[4:5, 0:channels] = shift[...]
    pv = vectors[...].T[:channels, :]
    GAIN1, GAIN2 = pv[:, 0:1], pv[:, 1:2]
    SUM_A, SUM_B, SUM_C, SUM_D, SUM_T = 13, 14, 15, 16, 17
    for i in range(5):
        column((8, 10, 9, 11, 12)[i], pv[:, i : i + 1])

    def first_sums(start):
        spread_lines(x, start)
        total = jnp.zeros((shard, LANES), F32)
        square = total
        for h in range(height):
            value = read_line(start, h)
            xs[pl.ds(start, shard), line(h)] = value.astype(BF16)
            total = total + value
            square = square + value * value
        cols[SUM_A, pl.ds(start, shard), :] = total
        cols[SUM_B, pl.ds(start, shard), :] = square
    chunked(first_sums)
    s0, s1 = lane_sum(cols[SUM_A]), lane_sum(cols[SUM_B])

    SLICE = 16
    COMMON = (shard // SLICE - 1) // 2 * SLICE

    def gather_start(full):
        mine = full.at[zero]
        near = go(mine, mine, {"zero": mate})
        far = []
        for i in range(COMMON // SLICE):
            at = pl.ds(pl.multiple_of(group * COMMON + i * SLICE, SLICE), SLICE)
            far.append(go(mine.at[at], mine.at[at], {"zero": over}))
        at = pl.ds(2 * COMMON, shard - 2 * COMMON)
        far.append(go(mine.at[at], mine.at[at], {"zero": over}))
        return near, far

    def gather_pass(full, far):
        theirs = full.at[over]
        passed, crossed = [], []
        for i in range(COMMON // SLICE):
            at = pl.ds(pl.multiple_of(group * COMMON + i * SLICE, SLICE), SLICE)
            far[i].wait_recv()
            crossed.append(go(theirs.at[at], theirs.at[at], {"groups": 1 - group}))
            passed.append(go(theirs.at[at], theirs.at[at], {"zero": mate}))
        return passed, crossed

    def gather_rest(full, far, passed, crossed):
        theirs = full.at[over]
        far[-1].wait_recv()
        at = pl.ds(2 * COMMON, shard - 2 * COMMON)
        passed.append(go(theirs.at[at], theirs.at[at], {"zero": mate}))
        for i in range(COMMON // SLICE):
            at = pl.ds(pl.multiple_of((1 - group) * COMMON + i * SLICE, SLICE), SLICE)
            crossed[i].wait_recv()
            passed.append(go(theirs.at[at], theirs.at[at], {"zero": mate}))

    def gather_finish(near, passed):
        near.wait_recv()
        for copy in passed:
            copy.wait_recv()

    pl.semaphore_wait(barrier, rows - 1 + 3)
    stat0 = stat_start(0, s0, s1)
    near1, far1 = gather_start(wfull1)
    halo_a = halo_edges(1, xs)
    flatten(w2s, wfull2)

    def cot_fill(start):
        spread_lines(g, start)
        for h in range(height):
            value = read_line(start, h)
            gs[pl.ds(start, shard), line(h)] = value.astype(BF16)
            put(cot_slab, value, start, h + 1)
    chunked(cot_fill)
    halo_g = halo_edges(0, gs)

    moments(0, stat0, 0)

    def first_act(start):
        at = pl.ds(start, shard)
        for h in range(height):
            normed = (xs[at, line(h)].astype(F32) - cols[0, at, :]) * cols[1, at, :]
            normed1[at, line(h)] = normed
            pre = cols[8, at, :] * normed + cols[9, at, :]
            act = (pre / (1.0 + jnp.exp(-pre))).astype(BF16).astype(F32)
            put(act_slab, act, start, h + 1)
    chunked(first_act)

    def first_edge(at, value):
        pre = cols[8, at, :] * ((value - cols[0, at, :]) * cols[1, at, :]) + cols[9, at, :]
        return (pre / (1.0 + jnp.exp(-pre))).astype(BF16).astype(F32)
    halo_finish(1, halo_a, act_slab, first_edge)
    passed1, crossed1 = gather_pass(wfull1, far1)
    near2, far2 = gather_start(wfull2)
    halo_finish(0, halo_g, cot_slab)
    gather_rest(wfull1, far1, passed1, crossed1)
    passed2, crossed2 = gather_pass(wfull2, far2)
    gather_finish(near1, passed1)

    def conv(weights, slab):
        value = None
        for b in range(3):
            term = jnp.dot(
                weights(slice(b * band, b * band + used)),
                slab[:, b * LANES : b * LANES + cells],
                preferred_element_type=F32,
            )
            value = term if value is None else value + term
        return value

    def forward(full):
        return lambda at: full[:, :, at].reshape(channels, at.stop - at.start)

    rounded = (conv(forward(wfull1), act_slab) + cols[12][:, 0:1]).astype(BF16)
    hidden[...] = rounded
    halo_b = halo_edges(2, hidden)

    def second_sums(start):
        total = jnp.zeros((shard, LANES), F32)
        square = total
        for h in range(height):
            value = hidden[pl.ds(start, shard), line(h)].astype(F32)
            total = total + value
            square = square + value * value
        cols[SUM_A, pl.ds(start, shard), :] = total
        cols[SUM_B, pl.ds(start, shard), :] = square
    chunked(second_sums)
    stat1 = stat_start(1, lane_sum(cols[SUM_A]), lane_sum(cols[SUM_B]))

    def turn(full, wturn):
        for b in range(3):
            begin = (2 - b) * band
            turned = full[:, :, begin : begin + used].reshape(channels, used).T
            wturn[:, b * band : b * band + used] = jnp.concatenate(
                [turned[i * channels : (i + 1) * channels] for i in (2, 1, 0)], axis=1
            )

    gather_rest(wfull2, far2, passed2, crossed2)
    turn(wfull1, wturn1)
    gather_finish(near2, passed2)
    turn(wfull2, wturn2)
    back[...] = conv(lambda at: wturn2[:, at], cot_slab)
    moments(1, stat1, 2)

    def second_act(start):
        at = pl.ds(start, shard)
        sums = [jnp.zeros((shard, LANES), F32)] * 2
        for h in range(height):
            normed = (hidden[at, line(h)].astype(F32) - cols[2, at, :]) * cols[3, at, :]
            normed2[at, line(h)] = normed
            pre = cols[10, at, :] * normed + cols[11, at, :]
            q = 1.0 / (1.0 + jnp.exp(-pre))
            act = (pre * q).astype(BF16).astype(F32)
            slope = back[at, line(h)] * (q * (1.0 + pre * (1.0 - q)))
            back[at, line(h)] = slope
            sums = [sums[0] + slope * normed, sums[1] + slope]
            put(mid_slab, act, start, h + 1)
        cols[SUM_C, at, :] = sums[0]
        cols[SUM_D, at, :] = sums[1]
    chunked(second_act)
    gain_cross2, bias_sum2 = lane_sum(cols[SUM_C]), lane_sum(cols[SUM_D])
    stat2 = stat_start(2, GAIN2 * bias_sum2, GAIN2 * gain_cross2)

    def second_edge(at, value):
        pre = cols[10, at, :] * ((value - cols[2, at, :]) * cols[3, at, :]) + cols[11, at, :]
        return (pre * (1.0 / (1.0 + jnp.exp(-pre)))).astype(BF16).astype(F32)
    halo_finish(2, halo_b, mid_slab, second_edge)

    last_row = rows - 1
    nearer = jnp.where(row < rows // 2, 0, 1)

    def weight_grad(stream, cot, slab):
        which, b, first, last = stream
        value = lax.dot_general(
            cot[...], slab[first:last, b * LANES : b * LANES + cells], (((1,), (1,)), ((), ())),
            preferred_element_type=F32,
        )
        part[which, :, :, b * band + first : b * band + last] = value.astype(BF16).reshape(
            blocks, shard, last - first
        )
        at = extent(stream)
        return [
            go(part.at[which, over_mate, :, at], core_in.at[which, 1, :, at], {"zero": mate}),
            go(part.at[which, mate, :, at], core_in.at[which, 0, :, at], {"zero": mate}),
        ]

    def extent(stream):
        _, b, first, last = stream
        return slice(b * band + first, b * band + -(-last // LANES) * LANES)

    def reduce_core(stream, copies):
        which, at = stream[0], extent(stream)
        copies[0].wait_recv()
        core_keep[which, :, at] = (
            part[which, over, :, at].astype(F32) + core_in[which, 1, :, at].astype(F32)
        ).astype(BF16)
        return copies[1], go(core_keep.at[which, :, at], x_in.at[which, :, at], {"zero": over})

    def reduce_over(stream, copies):
        which, at = stream[0], extent(stream)
        for copy in copies:
            copy.wait_recv()
        value = (
            part[which, zero, :, at].astype(F32)
            + core_in[which, 0, :, at].astype(F32)
            + x_in[which, :, at].astype(F32)
        )
        own[which, :, at] = value.astype(BF16)
        i = number()
        number()
        links = []
        for way in (nearer, 1 - nearer):
            links.append(pltpu.make_async_remote_copy(
                src_ref=chain_out.at[way, which, :, at],
                dst_ref=chain_in.at[way, which, :, at],
                send_sem=send.at[i + way], recv_sem=recv.at[i + way],
                device_id={"rows": jnp.clip(row + 1 - 2 * way, 0, last_row)}, device_id_type=MESH,
            ))
        arrives = [jnp.where(way == 0, row > 0, row < last_row) for way in (nearer, 1 - nearer)]
        leaves = [jnp.where(way == 0, row < last_row, row > 0) for way in (nearer, 1 - nearer)]
        for k, way in enumerate((nearer, 1 - nearer)):
            @pl.when(leaves[k] & jnp.logical_not(arrives[k]))
            def _(k=k, way=way):
                chain_out[way, which, :, at] = value.astype(chain_out.dtype)
                links[k].start()
        return links, arrives, leaves

    def chain_step(stream, state, k):
        which, at = stream[0], extent(stream)
        links, arrives, leaves = state
        way = (nearer, 1 - nearer)[k]

        @pl.when(leaves[k] & arrives[k])
        def _():
            links[k].wait_recv()
            chain_out[way, which, :, at] = (
                chain_in[way, which, :, at].astype(F32) + own[which, :, at].astype(F32)
            ).astype(chain_out.dtype)
            links[k].start()
        return state

    def chain_finish(stream, state):
        which, at = stream[0], extent(stream)
        links, arrives, leaves = state
        flat[which, :, at] = own[which, :, at].astype(F32)
        for k, way in enumerate((nearer, 1 - nearer)):
            @pl.when(arrives[k])
            def _(k=k, way=way):
                @pl.when(jnp.logical_not(leaves[k]))
                def _():
                    links[k].wait_recv()
                flat[which, :, at] += chain_in[way, which, :, at].astype(F32)

            @pl.when(leaves[k])
            def _(k=k):
                links[k].wait_send()

    def unpack(which, b, target):
        for i in range(bands):
            tap = bands * b + i
            dw_stage[which, tap] = flat[which, :, b * band + i * channels : b * band + (i + 1) * channels]
        at = pl.ds(bands * b, bands)
        store_out(dw_stage.at[which, at], target.at[at])

    WIDTH = 4 * LANES
    pieces = [
        (b, first, min(first + WIDTH, used)) for b in range(3) for first in range(0, used, WIDTH)
    ]
    count = len(pieces)
    streams = [(1, *piece) for piece in pieces] + [(0, *piece) for piece in pieces]
    state = {}

    def grad(k, cot, slab):
        state[k] = weight_grad(streams[k], cot, slab)

    def core_step(k):
        state[k] = reduce_core(streams[k], state[k])

    def advance(kind, k):
        if kind == 0:
            state[k] = reduce_over(streams[k], state[k])
        elif kind < 3:
            state[k] = chain_step(streams[k], state[k], kind - 1)
        else:
            chain_finish(streams[k], state[k])
            which, b, _, end = streams[k]
            if end == used:
                unpack(which, b, dw2 if which else dw1)

    events = sorted(
        (FIRST + PACE * k + HOP * kind, k, kind) for k in range(2 * count) for kind in range(4)
    )

    def drain(until):
        while events and events[0][0] <= until:
            _, k, kind = events.pop(0)
            advance(kind, k)

    LAG = 2
    for k in range(count):
        grad(k, gs, mid_slab)
        if k >= LAG:
            core_step(k - LAG)

    average, cross = stat_finish(2, stat2)
    column(4, average)
    column(5, cross)
    core_step(count - 2)

    def hidden_back(start):
        at = pl.ds(start, shard)
        total = jnp.zeros((shard, LANES), F32)
        for h in range(height):
            value = cols[3, at, :] * (
                cols[10, at, :] * back[at, line(h)]
                - cols[4, at, :]
                - normed2[at, line(h)] * cols[5, at, :]
            )
            total = total + value
            rounded = value.astype(BF16)
            hgrad[at, line(h)] = rounded
            put(cot_slab, rounded.astype(F32), start, h + 1)
        cols[SUM_T, at, :] = total
    chunked(hidden_back)
    halo_h = halo_edges(3, hgrad)
    core_step(count - 1)
    time_sum = lane_sum(cols[SUM_T])
    now = 4.5
    for k in range(count):
        grad(count + k, hgrad, act_slab)
        if k >= LAG:
            core_step(count + k - LAG)
        now += 0.4
        drain(now)
    core_step(2 * count - 2)
    halo_finish(3, halo_h, cot_slab)
    core_step(2 * count - 1)
    drain(now + 0.5)
    back[...] = conv(lambda at: wturn1[:, at], cot_slab)
    drain(now + 3.0)

    def first_slope(start):
        at = pl.ds(start, shard)
        sums = [jnp.zeros((shard, LANES), F32)] * 2
        for h in range(height):
            normed = normed1[at, line(h)]
            pre = cols[8, at, :] * normed + cols[9, at, :]
            q = 1.0 / (1.0 + jnp.exp(-pre))
            slope = back[at, line(h)] * (q * (1.0 + pre * (1.0 - q)))
            back[at, line(h)] = slope
            sums = [sums[0] + slope * normed, sums[1] + slope]
        cols[SUM_A, at, :] = sums[0]
        cols[SUM_B, at, :] = sums[1]
    chunked(first_slope)
    gain_cross1, bias_sum1 = lane_sum(cols[SUM_A]), lane_sum(cols[SUM_B])
    stat3 = stat_start(3, GAIN1 * bias_sum1, GAIN1 * gain_cross1)
    packed = jnp.zeros((channels, LANES), F32)
    for i, value in enumerate((time_sum, gain_cross1, bias_sum1, gain_cross2, bias_sum2)):
        packed = jnp.where(wide == i, value, packed)
    fill = jnp.zeros((tiny.shape[2] - channels, LANES), F32)
    tiny[row] = jnp.concatenate([packed, fill], axis=0).T[:8, :]
    tiny_rows = to_rows(tiny.at[row], tiny.at[row])
    drain(now + 4.2)

    value = conv(forward(wfull2), mid_slab)
    for h in range(height):
        lines[pl.ds(h, channels, stride=height), :] = xs[:, line(h)].astype(F32) + value[:, line(h)]

    def out_collect(start):
        collect_lines(out_stage, start)
    chunked(out_collect)
    store_out(out_stage, out)
    drain(now + 7.0)

    average, cross = stat_finish(3, stat3)
    column(6, average)
    column(7, cross)

    for copy in tiny_rows:
        copy.wait_recv()
    total = tiny[0]
    for i in range(1, rows):
        total = total + tiny[i]
    tiny_x[0] = total
    first_hop = go(tiny_x.at[0], tiny_x.at[1], {"zero": mate})

    def input_back(start):
        at = pl.ds(start, shard)
        for h in range(height):
            value = cols[1, at, :] * (
                cols[8, at, :] * back[at, line(h)]
                - cols[6, at, :]
                - normed1[at, line(h)] * cols[7, at, :]
            )
            write_line(start, h, gs[at, line(h)].astype(F32) + value)
        collect_lines(gin_stage, start)
    chunked(input_back)
    store_out(gin_stage, gin)
    drain(now + 8.5)

    first_hop.wait_recv()
    tiny_x[2] = total + tiny_x[1]
    second_hop = go(tiny_x.at[2], tiny_x.at[3], {"zero": over})
    drain(now + 12.0)
    second_hop.wait_recv()
    pick = lax.broadcasted_iota(jnp.int32, total.shape, 0)
    small[...] = jnp.where(pick == 0, total, tiny_x[2] + tiny_x[3])
    drain(1000.0)
    for copy in pending:
        copy.wait_send()
    for copy in stores:
        copy.wait()


def deliver(
    out, gin, small, dw1, dw2, out_to, gin_to, time_to, norms_to, dw1_to, dw2_to,
    fields, grads, get, put,
):
    moves = []
    for i, (src, held, dst) in enumerate((
        (out, fields.at[0], out_to), (gin, fields.at[1], gin_to),
        (dw2, grads.at[1], dw2_to), (dw1, grads.at[0], dw1_to),
    )):
        first = pltpu.make_async_copy(src, held, get.at[i])
        first.start()
        moves.append((first, pltpu.make_async_copy(held, dst, put.at[i])))
    channels = time_to.shape[1]
    time_to[...] = small[0:1, 0:channels]
    norms_to[...] = small[1:5, 0:channels]
    for first, then in moves:
        first.wait()
        then.start()
    for _, then in moves:
        then.wait()


FIRST, PACE, HOP = 5.4, 1.46, 3.4


def local(latents, time_shift, conv_first, conv_second, norm_gains, norm_biases, grad_output):
    _, channels, height, width = latents.shape
    cells = height * width
    shard, taps, _ = conv_first.shape
    rows = lax.axis_size("rows")
    blocks = channels // shard
    group = np.arange(channels) // (channels // NORM_GROUPS)
    pool = (group[None, :] == np.arange(NORM_GROUPS)[:, None]).astype(np.float32)
    used = taps // 3 * channels
    band = -(-used // LANES) * LANES
    span = 3 * band
    padded_cells = cells + 2 * LANES
    chain = BF16 if rows <= 8 else F32
    padded = -(-channels // LANES) * LANES
    vmem = pl.BlockSpec(memory_space=pltpu.VMEM)
    hbm = pl.BlockSpec(memory_space=pl.ANY)
    streams = 6 * -(-used // (4 * LANES))
    copies = 5 * (rows - 1) + 8 + 2 * 12 + streams * 5 + 2
    field = jax.ShapeDtypeStruct((channels, height, width), BF16)
    grads = jax.ShapeDtypeStruct((taps, shard, channels), F32)
    results = pl.pallas_call(
        block_kernel,
        out_shape=(field, field, jax.ShapeDtypeStruct((8, padded), F32), grads, grads),
        in_specs=[vmem] * 9,
        out_specs=(hbm, hbm, vmem, hbm, hbm),
        scratch_shapes=[
            pltpu.VMEM((used, padded_cells), BF16),
            pltpu.VMEM((used, padded_cells), BF16),
            pltpu.VMEM((used, padded_cells), BF16),
            pltpu.VMEM((blocks, shard, span), BF16),
            pltpu.VMEM((blocks, shard, span), BF16),
            pltpu.VMEM((channels, span), BF16),
            pltpu.VMEM((channels, span), BF16),
            pltpu.VMEM((channels, cells), BF16),
            pltpu.VMEM((channels, cells), BF16),
            pltpu.VMEM((channels, cells), BF16),
            pltpu.VMEM((channels, cells), F32),
            pltpu.VMEM((channels, cells), F32),
            pltpu.VMEM((channels, cells), F32),
            pltpu.VMEM((channels, cells), BF16),
            pltpu.VMEM((channels * height, LANES), F32),
            pltpu.VMEM((18, channels, LANES), F32),
            pltpu.VMEM((4, rows, NORM_GROUPS, LANES), F32),
            pltpu.VMEM((4, 2, channels, LANES), BF16),
            pltpu.VMEM((2, blocks, shard, span), BF16),
            pltpu.VMEM((2, 2, shard, span), BF16),
            pltpu.VMEM((2, shard, span), BF16),
            pltpu.VMEM((2, shard, span), BF16),
            pltpu.VMEM((2, shard, span), BF16),
            pltpu.VMEM((2, 2, shard, span), chain),
            pltpu.VMEM((2, 2, shard, span), chain),
            pltpu.VMEM((2, shard, span), F32),
            pltpu.VMEM((channels, height, LANES), BF16),
            pltpu.VMEM((channels, height, LANES), BF16),
            pltpu.VMEM((2, taps, shard, channels), F32),
            pltpu.VMEM((LANES, padded), F32),
            pltpu.VMEM((rows, 8, padded), F32),
            pltpu.VMEM((4, 8, padded), F32),
            pltpu.SemaphoreType.DMA((copies,)),
            pltpu.SemaphoreType.DMA((copies,)),
            pltpu.SemaphoreType.DMA((8,)),
        ],
        compiler_params=pltpu.CompilerParams(
            collective_id=0, has_side_effects=True, vmem_limit_bytes=60 * 1024 * 1024
        ),
    )(
        latents.reshape(channels, height, width),
        grad_output.reshape(channels, height, width),
        norm_gains,
        norm_biases,
        time_shift,
        jnp.transpose(conv_first, (1, 0, 2)),
        jnp.transpose(conv_second, (1, 0, 2)),
        jnp.asarray(pool),
        jnp.asarray(np.ascontiguousarray(pool.T)),
    )
    out, gin, time_grad, norms, dw1, dw2 = pl.pallas_call(
        deliver,
        out_shape=(
            field,
            field,
            jax.ShapeDtypeStruct((1, channels), F32),
            jax.ShapeDtypeStruct((4, channels), F32),
            grads,
            grads,
        ),
        in_specs=[hbm, hbm, vmem, hbm, hbm],
        out_specs=(hbm, hbm, vmem, vmem, hbm, hbm),
        scratch_shapes=[
            pltpu.VMEM((2, channels, height, width), BF16),
            pltpu.VMEM((2, taps, shard, channels), F32),
            pltpu.SemaphoreType.DMA((4,)),
            pltpu.SemaphoreType.DMA((4,)),
        ],
    )(*results)
    return (
        out.reshape(latents.shape),
        gin.reshape(latents.shape),
        time_grad,
        jnp.transpose(dw1, (1, 0, 2)),
        jnp.transpose(dw2, (1, 0, 2)),
        norms,
    )


def solution(mesh):
    placed = (
        P(("groups", "zero"), None, "rows", None),
        P(("groups", "zero"), None),
        P("zero", None, None),
        P("zero", None, None),
        P(),
        P(),
        P(("groups", "zero"), None, "rows", None),
    )
    return jax.shard_map(
        local,
        mesh=mesh,
        in_specs=placed,
        out_specs=(
            P(("groups", "zero"), None, "rows", None),
            P(("groups", "zero"), None, "rows", None),
            P(("groups", "zero"), None),
            P(("groups", "zero"), None, None),
            P(("groups", "zero"), None, None),
            P("groups", None),
        ),
        check_vma=False,
    )
```

```python
import jax
import jax.numpy as jnp
from jax import lax
from jax.experimental import pallas as pl
from jax.experimental.pallas import tpu as pltpu
from jax.sharding import PartitionSpec as P

NORM_GROUPS = 32
EPSILON = 1e-05
LANES = 128
F32 = jnp.float32
BF16 = jnp.bfloat16
MESH = pl.DeviceIdType.MESH


def block_kernel(
    x_hbm, g_hbm, gains, biases, shift, w1_hbm, w2_hbm,
    out, gin, small, dw1, dw2,
    x, g, w1s, w2s, pool, spread, act_slab, mid_slab, cot_slab, wfull1, wfull2, wturn1, wturn2,
    xs, gs, hidden, normed1, normed2, back, hgrad, lines, cols, stat, halo_in,
    part, core_in, core_keep, x_in, own, chain_in, chain_out, flat,
    out_stage, gin_stage, dw_stage, vectors, tiny, tiny_x,
    send, recv, local_sem, load_sem,
):
    loads = []
    for i, (src, dst) in enumerate(((w1_hbm, w1s), (x_hbm, x), (g_hbm, g), (w2_hbm, w2s))):
        copy = pltpu.make_async_copy(src, dst, load_sem.at[i])
        copy.start()
        loads.append(copy)
    channels, height, _ = x.shape
    cells = height * LANES
    taps, shard, _ = w1s.shape
    bands = taps // 3
    used = bands * channels
    band = wturn1.shape[1] // 3
    rows = lax.axis_size("rows")
    row = lax.axis_index("rows")
    zero = lax.axis_index("zero")
    group = lax.axis_index("groups")
    core = lax.rem(zero, 2)
    mate = zero + 1 - 2 * core
    over = lax.rem(zero + 2, 4)
    over_mate = lax.rem(mate + 2, 4)
    blocks = channels // shard
    members = float(channels // NORM_GROUPS * cells * rows)
    lane = lax.broadcasted_iota(jnp.int32, (shard, LANES), 1)
    wide = lax.broadcasted_iota(jnp.int32, (channels, LANES), 1)
    counter = [0]
    local_counter = [0]

    def number():
        counter[0] += 1
        return counter[0] - 1

    pending = []
    stores = []

    def store_out(src, dst):
        i = local_counter[0]
        local_counter[0] += 1
        copy = pltpu.make_async_copy(src, dst, local_sem.at[i])
        copy.start()
        stores.append(copy)

    def remote(src, dst, target):
        i = number()
        return pltpu.make_async_remote_copy(
            src_ref=src, dst_ref=dst, send_sem=send.at[i], recv_sem=recv.at[i],
            device_id=target, device_id_type=MESH,
        )

    def go(src, dst, target):
        copy = remote(src, dst, target)
        copy.start()
        pending.append(copy)
        return copy

    def to_rows(src, dst):
        return [go(src, dst, {"rows": lax.rem(row + d, rows)}) for d in range(1, rows)]

    def chunked(body):
        def step(c, _):
            body(pl.multiple_of(c * shard, shard))
            return 0
        lax.fori_loop(0, blocks, step, 0)

    def put(slab, value, start, p):
        left = jnp.where(lane == 0, 0.0, pltpu.roll(value, 1, 1)).astype(BF16)
        right = jnp.where(lane == LANES - 1, 0.0, pltpu.roll(value, LANES - 1, 1)).astype(BF16)
        for tx, shifted in enumerate((left, value.astype(BF16), right)):
            slab[pl.ds(start + tx * channels, shard), p * LANES : (p + 1) * LANES] = shifted

    def line(h):
        return slice(h * LANES, (h + 1) * LANES)

    def spread_lines(field, start):
        at = pl.ds(pl.multiple_of(start * height, shard * height), shard * height)
        lines[at, :] = field[pl.ds(start, shard)].astype(F32).reshape(shard * height, LANES)

    def read_line(start, h):
        return lines[pl.ds(start * height + h, shard, stride=height), :]

    def write_line(start, h, value):
        lines[pl.ds(start * height + h, shard, stride=height), :] = value

    def collect_lines(stage, start):
        at = pl.ds(pl.multiple_of(start * height, shard * height), shard * height)
        stage[pl.ds(start, shard)] = lines[at, :].reshape(shard, height, LANES).astype(BF16)

    def halo_start(stage, top, bottom):
        down = remote(bottom, halo_in.at[stage, 0], {"rows": lax.rem(row + 1, rows)})
        up = remote(top, halo_in.at[stage, 1], {"rows": lax.rem(row + rows - 1, rows)})

        @pl.when(row < rows - 1)
        def _():
            down.start()

        @pl.when(row > 0)
        def _():
            up.start()

        return down, up

    def halo_edges(stage, field):
        return halo_start(stage, field.at[:, line(0)], field.at[:, line(height - 1)])

    def halo_finish(stage, pair, slab, turned=None):
        down, up = pair

        @pl.when(row > 0)
        def _():
            down.wait_recv()
            up.wait_send()

        @pl.when(row < rows - 1)
        def _():
            up.wait_recv()
            down.wait_send()

        @pl.when(row == 0)
        def _():
            halo_in[stage, 0] = jnp.zeros((channels, LANES), BF16)

        @pl.when(row == rows - 1)
        def _():
            halo_in[stage, 1] = jnp.zeros((channels, LANES), BF16)

        def body(start):
            for side, p, inside in ((0, 0, row > 0), (1, height + 1, row < rows - 1)):
                value = halo_in[stage, side, pl.ds(start, shard), :].astype(F32)
                if turned is not None:
                    value = jnp.where(inside, turned(pl.ds(start, shard), value), 0.0)
                put(slab, value, start, p)
        chunked(body)

    def lane_sum(value):
        return jnp.sum(value, axis=1, keepdims=True)

    def stat_start(stage, first, second):
        packed = jnp.where(wide == 0, first, jnp.where(wide == 1, second, 0.0))
        stat[stage, row] = jnp.dot(
            pool[...], packed, precision=lax.Precision.HIGHEST, preferred_element_type=F32
        )
        return to_rows(stat.at[stage, row], stat.at[stage, row])

    def stat_finish(stage, copies):
        for copy in copies:
            copy.wait_recv()
        total = stat[stage, 0]
        for i in range(1, rows):
            total = total + stat[stage, i]
        wide_total = jnp.dot(
            spread[...], total, precision=lax.Precision.HIGHEST, preferred_element_type=F32
        ) / members
        return wide_total[:, 0:1], wide_total[:, 1:2]

    def column(i, value):
        cols[i] = jnp.broadcast_to(value, (channels, LANES))

    def moments(stage, copies, at):
        average, square = stat_finish(stage, copies)
        column(at, average)
        column(at + 1, lax.rsqrt(square - average * average + EPSILON))

    barrier = pltpu.get_barrier_semaphore()
    for d in range(1, rows):
        pl.semaphore_signal(
            barrier, inc=1, device_id={"rows": lax.rem(row + d, rows)}, device_id_type=MESH
        )
    for target in ({"zero": mate}, {"zero": over}, {"groups": 1 - group}):
        pl.semaphore_signal(barrier, inc=1, device_id=target, device_id_type=MESH)

    def flatten(shards, full):
        for b in range(3):
            full[zero, :, b * band : b * band + used] = jnp.concatenate(
                [shards[bands * b + i] for i in range(bands)], axis=1
            )

    members_of = channels // NORM_GROUPS
    offset = lax.broadcasted_iota(jnp.int32, pool.shape, 1) - members_of * lax.broadcasted_iota(
        jnp.int32, pool.shape, 0
    )
    pool[...] = jnp.where((offset >= 0) & (offset < members_of), 1.0, 0.0)
    offset = lax.broadcasted_iota(jnp.int32, spread.shape, 0) - members_of * lax.broadcasted_iota(
        jnp.int32, spread.shape, 1
    )
    spread[...] = jnp.where((offset >= 0) & (offset < members_of), 1.0, 0.0)
    vectors[...] = jnp.zeros_like(vectors)
    vectors[0:2, 0:channels] = gains[...]
    vectors[2:4, 0:channels] = biases[...]
    vectors[4:5, 0:channels] = shift[...]
    pv = vectors[...].T[:channels, :]
    GAIN1, GAIN2 = pv[:, 0:1], pv[:, 1:2]
    SUM_A, SUM_B, SUM_C, SUM_D, SUM_T = 13, 14, 15, 16, 17
    for i in range(5):
        column((8, 10, 9, 11, 12)[i], pv[:, i : i + 1])

    loads[0].wait()
    flatten(w1s, wfull1)
    loads[1].wait()

    def first_sums(start):
        spread_lines(x, start)
        total = jnp.zeros((shard, LANES), F32)
        square = total
        for h in range(height):
            value = read_line(start, h)
            xs[pl.ds(start, shard), line(h)] = value.astype(BF16)
            total = total + value
            square = square + value * value
        cols[SUM_A, pl.ds(start, shard), :] = total
        cols[SUM_B, pl.ds(start, shard), :] = square
    chunked(first_sums)
    s0, s1 = lane_sum(cols[SUM_A]), lane_sum(cols[SUM_B])

    SLICE = 16

    def shares(common):
        ours = [group * common + i * SLICE for i in range(common // SLICE)]
        theirs = [(1 - group) * common + i * SLICE for i in range(common // SLICE)]
        direct = list(range(2 * common, shard, SLICE))
        return ours, theirs, direct

    def strip(block, start):
        return block.at[pl.ds(start if isinstance(start, int) else pl.multiple_of(start, SLICE), SLICE)]

    def gather_start(full, common):
        mine = full.at[zero]
        near = go(mine, mine, {"zero": mate})
        ours, _, direct = shares(common)
        return near, [
            go(strip(mine, start), strip(mine, start), {"zero": over}) for start in ours + direct
        ]

    def gather_pass(full, common, far, passed, crossed):
        theirs = full.at[over]
        i = len(crossed)
        start = shares(common)[0][i]
        far[i].wait_recv()
        crossed.append(go(strip(theirs, start), strip(theirs, start), {"groups": 1 - group}))
        passed.append(go(strip(theirs, start), strip(theirs, start), {"zero": mate}))

    def gather_rest(full, common, far, passed, crossed):
        theirs = full.at[over]
        ours, others, direct = shares(common)
        arrivals = list(zip(far[len(ours):], direct)) + list(zip(crossed, others))
        for copy, start in arrivals:
            copy.wait_recv()
            passed.append(go(strip(theirs, start), strip(theirs, start), {"zero": mate}))

    def gather_finish(near, passed):
        near.wait_recv()
        for copy in passed:
            copy.wait_recv()

    pl.semaphore_wait(barrier, rows - 1 + 3)
    stat0 = stat_start(0, s0, s1)
    near1, far1 = gather_start(wfull1, COMMON1)
    passed1, crossed1, passed2, crossed2 = [], [], [], []
    halo_a = halo_edges(1, xs)
    loads[2].wait()
    loads[3].wait()
    flatten(w2s, wfull2)

    def cot_fill(start):
        spread_lines(g, start)
        for h in range(height):
            value = read_line(start, h)
            gs[pl.ds(start, shard), line(h)] = value.astype(BF16)
            put(cot_slab, value, start, h + 1)
    chunked(cot_fill)
    halo_g = halo_edges(0, gs)

    moments(0, stat0, 0)
    gather_pass(wfull1, COMMON1, far1, passed1, crossed1)

    def first_act(start):
        at = pl.ds(start, shard)
        for h in range(height):
            normed = (xs[at, line(h)].astype(F32) - cols[0, at, :]) * cols[1, at, :]
            normed1[at, line(h)] = normed
            pre = cols[8, at, :] * normed + cols[9, at, :]
            act = (pre / (1.0 + jnp.exp(-pre))).astype(BF16).astype(F32)
            put(act_slab, act, start, h + 1)
    chunked(first_act)

    def first_edge(at, value):
        pre = cols[8, at, :] * ((value - cols[0, at, :]) * cols[1, at, :]) + cols[9, at, :]
        return (pre / (1.0 + jnp.exp(-pre))).astype(BF16).astype(F32)
    halo_finish(1, halo_a, act_slab, first_edge)
    near2, far2 = gather_start(wfull2, COMMON2)
    halo_finish(0, halo_g, cot_slab)
    gather_rest(wfull1, COMMON1, far1, passed1, crossed1)
    gather_finish(near1, passed1)

    def conv(weights, slab, begin=0, end=cells):
        value = None
        for b in range(3):
            term = jnp.dot(
                weights(slice(b * band, b * band + used)),
                slab[:, b * LANES + begin : b * LANES + end],
                preferred_element_type=F32,
            )
            value = term if value is None else value + term
        return value

    def forward(full):
        return lambda at: full[:, :, at].reshape(channels, at.stop - at.start)

    rounded = (conv(forward(wfull1), act_slab) + cols[12][:, 0:1]).astype(BF16)
    hidden[...] = rounded
    halo_b = halo_edges(2, hidden)

    def second_sums(start):
        total = jnp.zeros((shard, LANES), F32)
        square = total
        for h in range(height):
            value = hidden[pl.ds(start, shard), line(h)].astype(F32)
            total = total + value
            square = square + value * value
        cols[SUM_A, pl.ds(start, shard), :] = total
        cols[SUM_B, pl.ds(start, shard), :] = square
    chunked(second_sums)
    stat1 = stat_start(1, lane_sum(cols[SUM_A]), lane_sum(cols[SUM_B]))

    def turn(full, wturn):
        for b in range(3):
            begin = (2 - b) * band
            turned = full[:, :, begin : begin + used].reshape(channels, used).T
            wturn[:, b * band : b * band + used] = jnp.concatenate(
                [turned[i * channels : (i + 1) * channels] for i in (2, 1, 0)], axis=1
            )

    for _ in range(COMMON2 // SLICE):
        gather_pass(wfull2, COMMON2, far2, passed2, crossed2)
    turn(wfull1, wturn1)
    moments(1, stat1, 2)

    def second_act(start):
        at = pl.ds(start, shard)
        for h in range(height):
            normed = (hidden[at, line(h)].astype(F32) - cols[2, at, :]) * cols[3, at, :]
            normed2[at, line(h)] = normed
            pre = cols[10, at, :] * normed + cols[11, at, :]
            act = (pre * (1.0 / (1.0 + jnp.exp(-pre)))).astype(BF16).astype(F32)
            put(mid_slab, act, start, h + 1)
    chunked(second_act)

    def second_edge(at, value):
        pre = cols[10, at, :] * ((value - cols[2, at, :]) * cols[3, at, :]) + cols[11, at, :]
        return (pre * (1.0 / (1.0 + jnp.exp(-pre)))).astype(BF16).astype(F32)
    halo_finish(2, halo_b, mid_slab, second_edge)
    gather_rest(wfull2, COMMON2, far2, passed2, crossed2)

    last_row = rows - 1
    nearer = jnp.where(row < rows // 2, 0, 1)

    def weight_grad(stream, cot, slab):
        which, b, first, last = stream
        value = lax.dot_general(
            cot[...], slab[first:last, b * LANES : b * LANES + cells], (((1,), (1,)), ((), ())),
            preferred_element_type=F32,
        )
        at = extent(stream)
        for unit in range(at.start, at.stop):
            lo = (unit - at.start) * LANES
            hi = min(lo + LANES, last - first)
            part[which, :, unit, :, 0 : hi - lo] = value[:, lo:hi].astype(BF16).reshape(
                blocks, shard, hi - lo
            )
        return [
            go(part.at[which, over_mate, at], core_in.at[which, 1, at], {"zero": mate}),
            go(part.at[which, mate, at], core_in.at[which, 0, at], {"zero": mate}),
        ]

    def extent(stream):
        _, b, first, last = stream
        begin = (b * band + first) // LANES
        return slice(begin, begin - (first - last) // LANES)

    def reduce_core(stream, copies):
        which, at = stream[0], extent(stream)
        copies[0].wait_recv()
        core_keep[which, at] = (
            part[which, over, at].astype(F32) + core_in[which, 1, at].astype(F32)
        ).astype(BF16)
        return copies[1], go(core_keep.at[which, at], x_in.at[which, at], {"zero": over})

    def reduce_over(stream, copies):
        which, at = stream[0], extent(stream)
        for copy in copies:
            copy.wait_recv()
        value = (
            part[which, zero, at].astype(F32)
            + core_in[which, 0, at].astype(F32)
            + x_in[which, at].astype(F32)
        )
        own[which, at] = value.astype(BF16)
        i = number()
        number()
        links = []
        for way in (nearer, 1 - nearer):
            links.append(pltpu.make_async_remote_copy(
                src_ref=chain_out.at[way, which, at],
                dst_ref=chain_in.at[way, which, at],
                send_sem=send.at[i + way], recv_sem=recv.at[i + way],
                device_id={"rows": jnp.clip(row + 1 - 2 * way, 0, last_row)}, device_id_type=MESH,
            ))
        arrives = [jnp.where(way == 0, row > 0, row < last_row) for way in (nearer, 1 - nearer)]
        leaves = [jnp.where(way == 0, row < last_row, row > 0) for way in (nearer, 1 - nearer)]
        for k, way in enumerate((nearer, 1 - nearer)):
            @pl.when(leaves[k] & jnp.logical_not(arrives[k]))
            def _(k=k, way=way):
                chain_out[way, which, at] = value.astype(chain_out.dtype)
                links[k].start()
        return links, arrives, leaves

    def chain_step(stream, state, k):
        which, at = stream[0], extent(stream)
        links, arrives, leaves = state
        way = (nearer, 1 - nearer)[k]

        @pl.when(leaves[k] & arrives[k])
        def _():
            links[k].wait_recv()
            chain_out[way, which, at] = (
                chain_in[way, which, at].astype(F32) + own[which, at].astype(F32)
            ).astype(chain_out.dtype)
            links[k].start()
        return state

    def chain_finish(stream, state):
        which, at = stream[0], extent(stream)
        links, arrives, leaves = state
        flat[which, at] = own[which, at].astype(F32)
        for k, way in enumerate((nearer, 1 - nearer)):
            @pl.when(arrives[k])
            def _(k=k, way=way):
                @pl.when(jnp.logical_not(leaves[k]))
                def _():
                    links[k].wait_recv()
                flat[which, at] += chain_in[way, which, at].astype(F32)

            @pl.when(leaves[k])
            def _(k=k):
                links[k].wait_send()

    def unpack(which, b, target):
        first = b * band // LANES
        whole = jnp.concatenate([flat[which, first + u] for u in range(band // LANES)], axis=1)
        for i in range(bands):
            dw_stage[which, bands * b + i] = whole[:, i * channels : (i + 1) * channels]
        at = pl.ds(bands * b, bands)
        store_out(dw_stage.at[which, at], target.at[at])

    def cut(widths):
        return [
            (b, first, min(first + width, used))
            for b, width in enumerate(widths) for first in range(0, used, width)
        ]

    streams = [(1, *piece) for piece in cut(SECOND)] + [(0, *piece) for piece in cut(FIRST)]
    count = len(cut(SECOND))
    state = {}

    def grad(k, cot, slab):
        state[k] = weight_grad(streams[k], cot, slab)

    def core_step(k):
        state[k] = reduce_core(streams[k], state[k])

    def advance(kind, k):
        if kind == 0:
            state[k] = reduce_over(streams[k], state[k])
        elif kind < 3:
            state[k] = chain_step(streams[k], state[k], kind - 1)
        else:
            chain_finish(streams[k], state[k])
            which, b, _, end = streams[k]
            if end == used:
                unpack(which, b, dw2 if which else dw1)

    events = []
    clock = START
    for k, (which, b, begin, end) in enumerate(streams):
        if k == count:
            clock = max(clock, RESTART)
        wire = PACE * -(-(end - begin) // LANES)
        clock += wire
        for kind in range(4):
            events.append((clock + kind * (wire + DELAY), k, kind))
    events.sort()

    def drain(until):
        while events and events[0][0] <= until:
            _, k, kind = events.pop(0)
            advance(kind, k)

    LAG = 2
    for k in range(count):
        grad(k, gs, mid_slab)
        if k >= LAG:
            core_step(k - LAG)

    gather_finish(near2, passed2)
    core_step(count - 2)
    turn(wfull2, wturn2)
    core_step(count - 1)
    half = cells // 2
    for begin in (0, half):
        back[:, begin : begin + half] = conv(
            lambda at: wturn2[:, at], cot_slab, begin, begin + half
        )
        drain(4.2 if begin == 0 else 5.4)

    def second_slope(start):
        at = pl.ds(start, shard)
        sums = [jnp.zeros((shard, LANES), F32)] * 2
        for h in range(height):
            normed = normed2[at, line(h)]
            pre = cols[10, at, :] * normed + cols[11, at, :]
            q = 1.0 / (1.0 + jnp.exp(-pre))
            slope = back[at, line(h)] * (q * (1.0 + pre * (1.0 - q)))
            back[at, line(h)] = slope
            sums = [sums[0] + slope * normed, sums[1] + slope]
        cols[SUM_C, at, :] = sums[0]
        cols[SUM_D, at, :] = sums[1]
    chunked(second_slope)
    gain_cross2, bias_sum2 = lane_sum(cols[SUM_C]), lane_sum(cols[SUM_D])
    stat2 = stat_start(2, GAIN2 * bias_sum2, GAIN2 * gain_cross2)
    drain(6.5)

    for begin in (0, half):
        value = conv(forward(wfull2), mid_slab, begin, begin + half)
        for i in range(half // LANES):
            h = begin // LANES + i
            lines[pl.ds(h, channels, stride=height), :] = (
                xs[:, line(h)].astype(F32) + value[:, line(i)]
            )
        drain(7.5 if begin == 0 else 8.5)

    def out_collect(start):
        collect_lines(out_stage, start)
    chunked(out_collect)
    store_out(out_stage, out)
    drain(9.0)

    average, cross = stat_finish(2, stat2)
    column(4, average)
    column(5, cross)

    def hidden_back(start):
        at = pl.ds(start, shard)
        total = jnp.zeros((shard, LANES), F32)
        for h in range(height):
            value = cols[3, at, :] * (
                cols[10, at, :] * back[at, line(h)]
                - cols[4, at, :]
                - normed2[at, line(h)] * cols[5, at, :]
            )
            total = total + value
            rounded = value.astype(BF16)
            hgrad[at, line(h)] = rounded
            put(cot_slab, rounded.astype(F32), start, h + 1)
        cols[SUM_T, at, :] = total
    chunked(hidden_back)
    drain(10.3)
    halo_h = halo_edges(3, hgrad)
    time_sum = lane_sum(cols[SUM_T])
    now = 10.5
    for k in range(count, len(streams)):
        grad(k, hgrad, act_slab)
        if k >= count + LAG:
            core_step(k - LAG)
        now += 0.1 * -(-(streams[k][3] - streams[k][2]) // LANES)
        drain(now)
    core_step(len(streams) - 2)
    halo_finish(3, halo_h, cot_slab)
    core_step(len(streams) - 1)
    drain(now + 0.5)
    for begin in (0, half):
        back[:, begin : begin + half] = conv(
            lambda at: wturn1[:, at], cot_slab, begin, begin + half
        )
        drain(now + (1.8 if begin == 0 else 3.0))

    def first_slope(start):
        at = pl.ds(start, shard)
        sums = [jnp.zeros((shard, LANES), F32)] * 2
        for h in range(height):
            normed = normed1[at, line(h)]
            pre = cols[8, at, :] * normed + cols[9, at, :]
            q = 1.0 / (1.0 + jnp.exp(-pre))
            slope = back[at, line(h)] * (q * (1.0 + pre * (1.0 - q)))
            back[at, line(h)] = slope
            sums = [sums[0] + slope * normed, sums[1] + slope]
        cols[SUM_A, at, :] = sums[0]
        cols[SUM_B, at, :] = sums[1]
    chunked(first_slope)
    drain(now + 3.8)
    gain_cross1, bias_sum1 = lane_sum(cols[SUM_A]), lane_sum(cols[SUM_B])
    stat3 = stat_start(3, GAIN1 * bias_sum1, GAIN1 * gain_cross1)
    packed = jnp.zeros((channels, LANES), F32)
    for i, value in enumerate((time_sum, gain_cross1, bias_sum1, gain_cross2, bias_sum2)):
        packed = jnp.where(wide == i, value, packed)
    fill = jnp.zeros((tiny.shape[2] - channels, LANES), F32)
    tiny[row] = jnp.concatenate([packed, fill], axis=0).T[:8, :]
    tiny_rows = to_rows(tiny.at[row], tiny.at[row])
    drain(now + 6.0)

    drain(now + 7.0)
    average, cross = stat_finish(3, stat3)
    column(6, average)
    column(7, cross)

    for copy in tiny_rows:
        copy.wait_recv()
    total = tiny[0]
    for i in range(1, rows):
        total = total + tiny[i]
    tiny_x[0] = total
    first_hop = go(tiny_x.at[0], tiny_x.at[1], {"zero": mate})

    def input_back(start):
        at = pl.ds(start, shard)
        for h in range(height):
            value = cols[1, at, :] * (
                cols[8, at, :] * back[at, line(h)]
                - cols[6, at, :]
                - normed1[at, line(h)] * cols[7, at, :]
            )
            write_line(start, h, gs[at, line(h)].astype(F32) + value)
        collect_lines(gin_stage, start)
    chunked(input_back)
    store_out(gin_stage, gin)
    drain(now + 8.5)

    first_hop.wait_recv()
    tiny_x[2] = total + tiny_x[1]
    second_hop = go(tiny_x.at[2], tiny_x.at[3], {"zero": over})
    drain(now + 12.0)
    second_hop.wait_recv()
    pick = lax.broadcasted_iota(jnp.int32, total.shape, 0)
    small[...] = jnp.where(pick == 0, total, tiny_x[2] + tiny_x[3])
    drain(events[-3][0])
    for copy in pending:
        copy.wait_send()
    drain(1000.0)
    for copy in stores:
        copy.wait()


def deliver(
    out, gin, small, dw1, dw2, out_to, gin_to, time_to, norms_to, dw1_to, dw2_to,
    fields, grads, get, put,
):
    moves = []
    for i, (src, held, dst) in enumerate((
        (out, fields.at[0], out_to), (gin, fields.at[1], gin_to),
        (dw2, grads.at[1], dw2_to), (dw1, grads.at[0], dw1_to),
    )):
        first = pltpu.make_async_copy(src, held, get.at[i])
        first.start()
        moves.append((first, pltpu.make_async_copy(held, dst, put.at[i])))
    channels = time_to.shape[1]
    time_to[...] = small[0:1, 0:channels]
    norms_to[...] = small[1:5, 0:channels]
    for first, then in moves:
        first.wait()
        then.start()
    for _, then in moves:
        then.wait()


SECOND = (4 * LANES, 4 * LANES, 4 * LANES)
FIRST = (4 * LANES, 4 * LANES, 4 * LANES)
COMMON1, COMMON2 = 16, 32
START, RESTART, PACE, DELAY = 2.6, 13.0, 0.4, 1.8


def local(latents, time_shift, conv_first, conv_second, norm_gains, norm_biases, grad_output):
    _, channels, height, width = latents.shape
    cells = height * width
    shard, taps, _ = conv_first.shape
    rows = lax.axis_size("rows")
    blocks = channels // shard
    used = taps // 3 * channels
    band = -(-used // LANES) * LANES
    span = 3 * band
    units = span // LANES
    padded_cells = cells + 2 * LANES
    chain = BF16 if rows <= 8 else F32
    padded = -(-channels // LANES) * LANES
    vmem = pl.BlockSpec(memory_space=pltpu.VMEM)
    hbm = pl.BlockSpec(memory_space=pl.ANY)
    streams = sum(-(-used // width) for width in SECOND + FIRST)
    copies = 5 * (rows - 1) + 8 + 2 * 18 + streams * 5 + 2
    field = jax.ShapeDtypeStruct((channels, height, width), BF16)
    grads = jax.ShapeDtypeStruct((taps, shard, channels), F32)
    results = pl.pallas_call(
        block_kernel,
        out_shape=(field, field, jax.ShapeDtypeStruct((8, padded), F32), grads, grads),
        in_specs=[hbm, hbm, vmem, vmem, vmem, hbm, hbm],
        out_specs=(hbm, hbm, vmem, hbm, hbm),
        scratch_shapes=[
            pltpu.VMEM((channels, height, width), BF16),
            pltpu.VMEM((channels, height, width), BF16),
            pltpu.VMEM((taps, shard, channels), BF16),
            pltpu.VMEM((taps, shard, channels), BF16),
            pltpu.VMEM((NORM_GROUPS, channels), F32),
            pltpu.VMEM((channels, NORM_GROUPS), F32),
            pltpu.VMEM((used, padded_cells), BF16),
            pltpu.VMEM((used, padded_cells), BF16),
            pltpu.VMEM((used, padded_cells), BF16),
            pltpu.VMEM((blocks, shard, span), BF16),
            pltpu.VMEM((blocks, shard, span), BF16),
            pltpu.VMEM((channels, span), BF16),
            pltpu.VMEM((channels, span), BF16),
            pltpu.VMEM((channels, cells), BF16),
            pltpu.VMEM((channels, cells), BF16),
            pltpu.VMEM((channels, cells), BF16),
            pltpu.VMEM((channels, cells), F32),
            pltpu.VMEM((channels, cells), F32),
            pltpu.VMEM((channels, cells), F32),
            pltpu.VMEM((channels, cells), BF16),
            pltpu.VMEM((channels * height, LANES), F32),
            pltpu.VMEM((18, channels, LANES), F32),
            pltpu.VMEM((4, rows, NORM_GROUPS, LANES), F32),
            pltpu.VMEM((4, 2, channels, LANES), BF16),
            pltpu.VMEM((2, blocks, units, shard, LANES), BF16),
            pltpu.VMEM((2, 2, units, shard, LANES), BF16),
            pltpu.VMEM((2, units, shard, LANES), BF16),
            pltpu.VMEM((2, units, shard, LANES), BF16),
            pltpu.VMEM((2, units, shard, LANES), BF16),
            pltpu.VMEM((2, 2, units, shard, LANES), chain),
            pltpu.VMEM((2, 2, units, shard, LANES), chain),
            pltpu.VMEM((2, units, shard, LANES), F32),
            pltpu.VMEM((channels, height, LANES), BF16),
            pltpu.VMEM((channels, height, LANES), BF16),
            pltpu.VMEM((2, taps, shard, channels), F32),
            pltpu.VMEM((LANES, padded), F32),
            pltpu.VMEM((rows, 8, padded), F32),
            pltpu.VMEM((4, 8, padded), F32),
            pltpu.SemaphoreType.DMA((copies,)),
            pltpu.SemaphoreType.DMA((copies,)),
            pltpu.SemaphoreType.DMA((8,)),
            pltpu.SemaphoreType.DMA((4,)),
        ],
        compiler_params=pltpu.CompilerParams(
            collective_id=0, has_side_effects=True, vmem_limit_bytes=60 * 1024 * 1024
        ),
    )(
        latents.reshape(channels, height, width),
        grad_output.reshape(channels, height, width),
        norm_gains,
        norm_biases,
        time_shift,
        jnp.transpose(conv_first, (1, 0, 2)),
        jnp.transpose(conv_second, (1, 0, 2)),
    )
    out, gin, time_grad, norms, dw1, dw2 = pl.pallas_call(
        deliver,
        out_shape=(
            field,
            field,
            jax.ShapeDtypeStruct((1, channels), F32),
            jax.ShapeDtypeStruct((4, channels), F32),
            grads,
            grads,
        ),
        in_specs=[hbm, hbm, vmem, hbm, hbm],
        out_specs=(hbm, hbm, vmem, vmem, hbm, hbm),
        scratch_shapes=[
            pltpu.VMEM((2, channels, height, width), BF16),
            pltpu.VMEM((2, taps, shard, channels), F32),
            pltpu.SemaphoreType.DMA((4,)),
            pltpu.SemaphoreType.DMA((4,)),
        ],
    )(*results)
    return (
        out.reshape(latents.shape),
        gin.reshape(latents.shape),
        time_grad,
        jnp.transpose(dw1, (1, 0, 2)),
        jnp.transpose(dw2, (1, 0, 2)),
        norms,
    )


def solution(mesh):
    placed = (
        P(("groups", "zero"), None, "rows", None),
        P(("groups", "zero"), None),
        P("zero", None, None),
        P("zero", None, None),
        P(),
        P(),
        P(("groups", "zero"), None, "rows", None),
    )
    return jax.shard_map(
        local,
        mesh=mesh,
        in_specs=placed,
        out_specs=(
            P(("groups", "zero"), None, "rows", None),
            P(("groups", "zero"), None, "rows", None),
            P(("groups", "zero"), None),
            P(("groups", "zero"), None, None),
            P(("groups", "zero"), None, None),
            P("groups", None),
        ),
        check_vma=False,
    )
```

```python
import jax
import jax.numpy as jnp
from jax import lax
from jax.experimental import pallas as pl
from jax.experimental.pallas import tpu as pltpu
from jax.sharding import PartitionSpec as P

NORM_GROUPS = 32
EPSILON = 1e-05
LANES = 128
F32 = jnp.float32
BF16 = jnp.bfloat16
MESH = pl.DeviceIdType.MESH


def block_kernel(
    x_hbm, g_hbm, gains, biases, shift, w1_hbm, w2_hbm,
    out, gin, small, dw1, dw2,
    x, g, w1s, w2s, pool, spread, act_slab, mid_slab, cot_slab, wfull1, wfull2, wturn1, wturn2,
    xs, gs, hidden, normed1, normed2, back, hgrad, lines, cols, stat, halo_in,
    part, core_in, core_keep, x_in, own, chain_in, chain_out, flat,
    out_stage, gin_stage, dw_stage, vectors, tiny, tiny_x,
    send, recv, local_sem, load_sem,
):
    loads = []
    for i, (src, dst) in enumerate(((w1_hbm, w1s), (x_hbm, x), (g_hbm, g), (w2_hbm, w2s))):
        copy = pltpu.make_async_copy(src, dst, load_sem.at[i])
        copy.start()
        loads.append(copy)
    channels, height, _ = x.shape
    cells = height * LANES
    taps, shard, _ = w1s.shape
    bands = taps // 3
    used = bands * channels
    band = wturn1.shape[1] // 3
    rows = lax.axis_size("rows")
    row = lax.axis_index("rows")
    zero = lax.axis_index("zero")
    group = lax.axis_index("groups")
    core = lax.rem(zero, 2)
    mate = zero + 1 - 2 * core
    over = lax.rem(zero + 2, 4)
    over_mate = lax.rem(mate + 2, 4)
    blocks = channels // shard
    members = float(channels // NORM_GROUPS * cells * rows)
    lane = lax.broadcasted_iota(jnp.int32, (shard, LANES), 1)
    wide = lax.broadcasted_iota(jnp.int32, (channels, LANES), 1)
    counter = [0]
    local_counter = [0]

    def number():
        counter[0] += 1
        return counter[0] - 1

    pending = []
    stores = []

    def store_out(src, dst):
        i = local_counter[0]
        local_counter[0] += 1
        copy = pltpu.make_async_copy(src, dst, local_sem.at[i])
        copy.start()
        stores.append(copy)

    def remote(src, dst, target):
        i = number()
        return pltpu.make_async_remote_copy(
            src_ref=src, dst_ref=dst, send_sem=send.at[i], recv_sem=recv.at[i],
            device_id=target, device_id_type=MESH,
        )

    def go(src, dst, target):
        copy = remote(src, dst, target)
        copy.start()
        pending.append(copy)
        return copy

    def to_rows(src, dst):
        return [go(src, dst, {"rows": lax.rem(row + d, rows)}) for d in range(1, rows)]

    def chunked(body):
        def step(c, _):
            body(pl.multiple_of(c * shard, shard))
            return 0
        lax.fori_loop(0, blocks, step, 0)

    def put(slab, value, start, p):
        left = jnp.where(lane == 0, 0.0, pltpu.roll(value, 1, 1)).astype(BF16)
        right = jnp.where(lane == LANES - 1, 0.0, pltpu.roll(value, LANES - 1, 1)).astype(BF16)
        for tx, shifted in enumerate((left, value.astype(BF16), right)):
            slab[pl.ds(start + tx * channels, shard), p * LANES : (p + 1) * LANES] = shifted

    def line(h):
        return slice(h * LANES, (h + 1) * LANES)

    def spread_lines(field, start):
        at = pl.ds(pl.multiple_of(start * height, shard * height), shard * height)
        lines[at, :] = field[pl.ds(start, shard)].astype(F32).reshape(shard * height, LANES)

    def read_line(start, h):
        return lines[pl.ds(start * height + h, shard, stride=height), :]

    def write_line(start, h, value):
        lines[pl.ds(start * height + h, shard, stride=height), :] = value

    def collect_lines(stage, start):
        at = pl.ds(pl.multiple_of(start * height, shard * height), shard * height)
        stage[pl.ds(start, shard)] = lines[at, :].reshape(shard, height, LANES).astype(BF16)

    def halo_start(stage, top, bottom):
        down = remote(bottom, halo_in.at[stage, 0], {"rows": lax.rem(row + 1, rows)})
        up = remote(top, halo_in.at[stage, 1], {"rows": lax.rem(row + rows - 1, rows)})

        @pl.when(row < rows - 1)
        def _():
            down.start()

        @pl.when(row > 0)
        def _():
            up.start()

        return down, up

    def halo_edges(stage, field):
        return halo_start(stage, field.at[:, line(0)], field.at[:, line(height - 1)])

    def halo_finish(stage, pair, slab, turned=None):
        down, up = pair

        @pl.when(row > 0)
        def _():
            down.wait_recv()
            up.wait_send()

        @pl.when(row < rows - 1)
        def _():
            up.wait_recv()
            down.wait_send()

        @pl.when(row == 0)
        def _():
            halo_in[stage, 0] = jnp.zeros((channels, LANES), BF16)

        @pl.when(row == rows - 1)
        def _():
            halo_in[stage, 1] = jnp.zeros((channels, LANES), BF16)

        def body(start):
            for side, p, inside in ((0, 0, row > 0), (1, height + 1, row < rows - 1)):
                value = halo_in[stage, side, pl.ds(start, shard), :].astype(F32)
                if turned is not None:
                    value = jnp.where(inside, turned(pl.ds(start, shard), value), 0.0)
                put(slab, value, start, p)
        chunked(body)

    def lane_sum(value):
        return jnp.sum(value, axis=1, keepdims=True)

    def stat_start(stage, first, second):
        packed = jnp.where(wide == 0, first, jnp.where(wide == 1, second, 0.0))
        stat[stage, row] = jnp.dot(
            pool[...], packed, precision=lax.Precision.HIGHEST, preferred_element_type=F32
        )
        return to_rows(stat.at[stage, row], stat.at[stage, row])

    def stat_finish(stage, copies):
        for copy in copies:
            copy.wait_recv()
        total = stat[stage, 0]
        for i in range(1, rows):
            total = total + stat[stage, i]
        wide_total = jnp.dot(
            spread[...], total, precision=lax.Precision.HIGHEST, preferred_element_type=F32
        ) / members
        return wide_total[:, 0:1], wide_total[:, 1:2]

    def column(i, value):
        cols[i] = jnp.broadcast_to(value, (channels, LANES))

    def moments(stage, copies, at):
        average, square = stat_finish(stage, copies)
        column(at, average)
        column(at + 1, lax.rsqrt(square - average * average + EPSILON))

    barrier = pltpu.get_barrier_semaphore()
    for d in range(1, rows):
        pl.semaphore_signal(
            barrier, inc=1, device_id={"rows": lax.rem(row + d, rows)}, device_id_type=MESH
        )
    for target in ({"zero": mate}, {"zero": over}, {"groups": 1 - group}):
        pl.semaphore_signal(barrier, inc=1, device_id=target, device_id_type=MESH)

    def flatten(shards, full):
        for b in range(3):
            full[zero, :, b * band : b * band + used] = jnp.concatenate(
                [shards[bands * b + i] for i in range(bands)], axis=1
            )

    members_of = channels // NORM_GROUPS
    offset = lax.broadcasted_iota(jnp.int32, pool.shape, 1) - members_of * lax.broadcasted_iota(
        jnp.int32, pool.shape, 0
    )
    pool[...] = jnp.where((offset >= 0) & (offset < members_of), 1.0, 0.0)
    offset = lax.broadcasted_iota(jnp.int32, spread.shape, 0) - members_of * lax.broadcasted_iota(
        jnp.int32, spread.shape, 1
    )
    spread[...] = jnp.where((offset >= 0) & (offset < members_of), 1.0, 0.0)
    vectors[...] = jnp.zeros_like(vectors)
    vectors[0:2, 0:channels] = gains[...]
    vectors[2:4, 0:channels] = biases[...]
    vectors[4:5, 0:channels] = shift[...]
    pv = vectors[...].T[:channels, :]
    GAIN1, GAIN2 = pv[:, 0:1], pv[:, 1:2]
    SUM_A, SUM_B, SUM_C, SUM_D, SUM_T = 13, 14, 15, 16, 17
    for i in range(5):
        column((8, 10, 9, 11, 12)[i], pv[:, i : i + 1])

    loads[0].wait()
    flatten(w1s, wfull1)
    loads[1].wait()

    def first_sums(start):
        spread_lines(x, start)
        total = jnp.zeros((shard, LANES), F32)
        square = total
        for h in range(height):
            value = read_line(start, h)
            xs[pl.ds(start, shard), line(h)] = value.astype(BF16)
            total = total + value
            square = square + value * value
        cols[SUM_A, pl.ds(start, shard), :] = total
        cols[SUM_B, pl.ds(start, shard), :] = square
    chunked(first_sums)
    s0, s1 = lane_sum(cols[SUM_A]), lane_sum(cols[SUM_B])

    SLICE = 16

    def shares(common):
        ours = [group * common + i * SLICE for i in range(common // SLICE)]
        theirs = [(1 - group) * common + i * SLICE for i in range(common // SLICE)]
        direct = list(range(2 * common, shard, SLICE))
        return ours, theirs, direct

    def strip(block, start):
        return block.at[pl.ds(start if isinstance(start, int) else pl.multiple_of(start, SLICE), SLICE)]

    def gather_start(full, common):
        mine = full.at[zero]
        near = go(mine, mine, {"zero": mate})
        ours, _, direct = shares(common)
        return near, [
            go(strip(mine, start), strip(mine, start), {"zero": over}) for start in ours + direct
        ]

    def gather_pass(full, common, far, passed, crossed):
        theirs = full.at[over]
        i = len(crossed)
        start = shares(common)[0][i]
        far[i].wait_recv()
        crossed.append(go(strip(theirs, start), strip(theirs, start), {"groups": 1 - group}))
        passed.append(go(strip(theirs, start), strip(theirs, start), {"zero": mate}))

    def gather_rest(full, common, far, passed, crossed):
        theirs = full.at[over]
        ours, others, direct = shares(common)
        arrivals = list(zip(far[len(ours):], direct)) + list(zip(crossed, others))
        for copy, start in arrivals:
            copy.wait_recv()
            passed.append(go(strip(theirs, start), strip(theirs, start), {"zero": mate}))

    def gather_finish(near, passed):
        near.wait_recv()
        for copy in passed:
            copy.wait_recv()

    pl.semaphore_wait(barrier, rows - 1 + 3)
    stat0 = stat_start(0, s0, s1)
    near1, far1 = gather_start(wfull1, COMMON1)
    passed1, crossed1, passed2, crossed2 = [], [], [], []
    halo_a = halo_edges(1, xs)
    loads[2].wait()
    loads[3].wait()
    flatten(w2s, wfull2)

    def cot_fill(start):
        spread_lines(g, start)
        for h in range(height):
            value = read_line(start, h)
            gs[pl.ds(start, shard), line(h)] = value.astype(BF16)
            put(cot_slab, value, start, h + 1)
    chunked(cot_fill)
    halo_g = halo_edges(0, gs)

    moments(0, stat0, 0)
    gather_pass(wfull1, COMMON1, far1, passed1, crossed1)

    def first_act(start):
        at = pl.ds(start, shard)
        for h in range(height):
            normed = (xs[at, line(h)].astype(F32) - cols[0, at, :]) * cols[1, at, :]
            normed1[at, line(h)] = normed
            pre = cols[8, at, :] * normed + cols[9, at, :]
            act = (pre / (1.0 + jnp.exp(-pre))).astype(BF16).astype(F32)
            put(act_slab, act, start, h + 1)
    chunked(first_act)

    def first_edge(at, value):
        pre = cols[8, at, :] * ((value - cols[0, at, :]) * cols[1, at, :]) + cols[9, at, :]
        return (pre / (1.0 + jnp.exp(-pre))).astype(BF16).astype(F32)
    halo_finish(1, halo_a, act_slab, first_edge)
    gather_pass(wfull1, COMMON1, far1, passed1, crossed1)
    near2, far2 = gather_start(wfull2, COMMON2)
    halo_finish(0, halo_g, cot_slab)
    gather_rest(wfull1, COMMON1, far1, passed1, crossed1)
    gather_finish(near1, passed1)

    def conv(weights, slab, begin=0, end=cells):
        value = None
        for b in range(3):
            term = jnp.dot(
                weights(slice(b * band, b * band + used)),
                slab[:, b * LANES + begin : b * LANES + end],
                preferred_element_type=F32,
            )
            value = term if value is None else value + term
        return value

    def forward(full):
        return lambda at: full[:, :, at].reshape(channels, at.stop - at.start)

    rounded = (conv(forward(wfull1), act_slab) + cols[12][:, 0:1]).astype(BF16)
    hidden[...] = rounded
    halo_b = halo_edges(2, hidden)

    def second_sums(start):
        total = jnp.zeros((shard, LANES), F32)
        square = total
        for h in range(height):
            value = hidden[pl.ds(start, shard), line(h)].astype(F32)
            total = total + value
            square = square + value * value
        cols[SUM_A, pl.ds(start, shard), :] = total
        cols[SUM_B, pl.ds(start, shard), :] = square
    chunked(second_sums)
    stat1 = stat_start(1, lane_sum(cols[SUM_A]), lane_sum(cols[SUM_B]))

    def turn(full, wturn):
        for b in range(3):
            begin = (2 - b) * band
            turned = full[:, :, begin : begin + used].reshape(channels, used).T
            wturn[:, b * band : b * band + used] = jnp.concatenate(
                [turned[i * channels : (i + 1) * channels] for i in (2, 1, 0)], axis=1
            )

    for _ in range(COMMON2 // SLICE):
        gather_pass(wfull2, COMMON2, far2, passed2, crossed2)
    turn(wfull1, wturn1)
    moments(1, stat1, 2)

    def second_act(start):
        at = pl.ds(start, shard)
        for h in range(height):
            normed = (hidden[at, line(h)].astype(F32) - cols[2, at, :]) * cols[3, at, :]
            normed2[at, line(h)] = normed
            pre = cols[10, at, :] * normed + cols[11, at, :]
            act = (pre * (1.0 / (1.0 + jnp.exp(-pre)))).astype(BF16).astype(F32)
            put(mid_slab, act, start, h + 1)
    chunked(second_act)

    def second_edge(at, value):
        pre = cols[10, at, :] * ((value - cols[2, at, :]) * cols[3, at, :]) + cols[11, at, :]
        return (pre * (1.0 / (1.0 + jnp.exp(-pre)))).astype(BF16).astype(F32)
    halo_finish(2, halo_b, mid_slab, second_edge)
    gather_rest(wfull2, COMMON2, far2, passed2, crossed2)

    last_row = rows - 1
    nearer = jnp.where(row < rows // 2, 0, 1)

    def weight_grad(stream, cot, slab):
        which, b, first, last = stream
        value = lax.dot_general(
            cot[...], slab[first:last, b * LANES : b * LANES + cells], (((1,), (1,)), ((), ())),
            preferred_element_type=F32,
        )
        at = extent(stream)
        for unit in range(at.start, at.stop):
            lo = (unit - at.start) * LANES
            hi = min(lo + LANES, last - first)
            part[which, :, unit, :, 0 : hi - lo] = value[:, lo:hi].astype(BF16).reshape(
                blocks, shard, hi - lo
            )
        return [
            go(part.at[which, over_mate, at], core_in.at[which, 1, at], {"zero": mate}),
            go(part.at[which, mate, at], core_in.at[which, 0, at], {"zero": mate}),
        ]

    def extent(stream):
        _, b, first, last = stream
        begin = (b * band + first) // LANES
        return slice(begin, begin - (first - last) // LANES)

    def reduce_core(stream, copies):
        which, at = stream[0], extent(stream)
        copies[0].wait_recv()
        core_keep[which, at] = (
            part[which, over, at].astype(F32) + core_in[which, 1, at].astype(F32)
        ).astype(BF16)
        return copies[1], go(core_keep.at[which, at], x_in.at[which, at], {"zero": over})

    def reduce_over(stream, copies):
        which, at = stream[0], extent(stream)
        for copy in copies:
            copy.wait_recv()
        value = (
            part[which, zero, at].astype(F32)
            + core_in[which, 0, at].astype(F32)
            + x_in[which, at].astype(F32)
        )
        own[which, at] = value.astype(BF16)
        i = number()
        number()
        links = []
        for way in (nearer, 1 - nearer):
            links.append(pltpu.make_async_remote_copy(
                src_ref=chain_out.at[way, which, at],
                dst_ref=chain_in.at[way, which, at],
                send_sem=send.at[i + way], recv_sem=recv.at[i + way],
                device_id={"rows": jnp.clip(row + 1 - 2 * way, 0, last_row)}, device_id_type=MESH,
            ))
        arrives = [jnp.where(way == 0, row > 0, row < last_row) for way in (nearer, 1 - nearer)]
        leaves = [jnp.where(way == 0, row < last_row, row > 0) for way in (nearer, 1 - nearer)]
        for k, way in enumerate((nearer, 1 - nearer)):
            @pl.when(leaves[k] & jnp.logical_not(arrives[k]))
            def _(k=k, way=way):
                chain_out[way, which, at] = value.astype(chain_out.dtype)
                links[k].start()
        return links, arrives, leaves

    def chain_step(stream, state, k):
        which, at = stream[0], extent(stream)
        links, arrives, leaves = state
        way = (nearer, 1 - nearer)[k]

        @pl.when(leaves[k] & arrives[k])
        def _():
            links[k].wait_recv()
            chain_out[way, which, at] = (
                chain_in[way, which, at].astype(F32) + own[which, at].astype(F32)
            ).astype(chain_out.dtype)
            links[k].start()
        return state

    def chain_finish(stream, state):
        which, at = stream[0], extent(stream)
        links, arrives, leaves = state
        flat[which, at] = own[which, at].astype(F32)
        for k, way in enumerate((nearer, 1 - nearer)):
            @pl.when(arrives[k])
            def _(k=k, way=way):
                @pl.when(jnp.logical_not(leaves[k]))
                def _():
                    links[k].wait_recv()
                flat[which, at] += chain_in[way, which, at].astype(F32)

            @pl.when(leaves[k])
            def _(k=k):
                links[k].wait_send()

    def unpack(which, b, target):
        first = b * band // LANES
        whole = jnp.concatenate([flat[which, first + u] for u in range(band // LANES)], axis=1)
        for i in range(bands):
            dw_stage[which, bands * b + i] = whole[:, i * channels : (i + 1) * channels]
        at = pl.ds(bands * b, bands)
        store_out(dw_stage.at[which, at], target.at[at])

    def cut(widths):
        return [
            (b, first, min(first + width, used))
            for b, width in enumerate(widths) for first in range(0, used, width)
        ]

    streams = [(1, *piece) for piece in cut(SECOND)] + [(0, *piece) for piece in cut(FIRST)]
    count = len(cut(SECOND))
    state = {}

    def grad(k, cot, slab):
        state[k] = weight_grad(streams[k], cot, slab)

    def core_step(k):
        state[k] = reduce_core(streams[k], state[k])

    def advance(kind, k):
        if kind == 0:
            state[k] = reduce_over(streams[k], state[k])
        elif kind < 3:
            state[k] = chain_step(streams[k], state[k], kind - 1)
        else:
            chain_finish(streams[k], state[k])
            which, b, _, end = streams[k]
            if end == used:
                unpack(which, b, dw2 if which else dw1)

    events = []
    clock = START
    for k, (which, b, begin, end) in enumerate(streams):
        if k == count:
            clock = max(clock, RESTART)
        wire = PACE * -(-(end - begin) // LANES)
        clock += wire
        for kind in range(4):
            events.append((clock + kind * (wire + DELAY), k, kind))
    events.sort()

    def drain(until):
        while events and events[0][0] <= until:
            _, k, kind = events.pop(0)
            advance(kind, k)

    LAG = 2
    for k in range(count):
        grad(k, gs, mid_slab)
        if k >= LAG:
            core_step(k - LAG)

    core_step(count - 2)
    gather_finish(near2, passed2)
    turn(wfull2, wturn2)
    core_step(count - 1)
    half = cells // 2
    for begin in (0, half):
        back[:, begin : begin + half] = conv(
            lambda at: wturn2[:, at], cot_slab, begin, begin + half
        )
        drain(4.2 if begin == 0 else 5.4)

    def second_slope(start):
        at = pl.ds(start, shard)
        sums = [jnp.zeros((shard, LANES), F32)] * 2
        for h in range(height):
            normed = normed2[at, line(h)]
            pre = cols[10, at, :] * normed + cols[11, at, :]
            q = 1.0 / (1.0 + jnp.exp(-pre))
            slope = back[at, line(h)] * (q * (1.0 + pre * (1.0 - q)))
            back[at, line(h)] = slope
            sums = [sums[0] + slope * normed, sums[1] + slope]
        cols[SUM_C, at, :] = sums[0]
        cols[SUM_D, at, :] = sums[1]
    chunked(second_slope)
    gain_cross2, bias_sum2 = lane_sum(cols[SUM_C]), lane_sum(cols[SUM_D])
    stat2 = stat_start(2, GAIN2 * bias_sum2, GAIN2 * gain_cross2)
    drain(6.5)

    for begin in (0, half):
        value = conv(forward(wfull2), mid_slab, begin, begin + half)
        for i in range(half // LANES):
            h = begin // LANES + i
            lines[pl.ds(h, channels, stride=height), :] = (
                xs[:, line(h)].astype(F32) + value[:, line(i)]
            )
        drain(7.5 if begin == 0 else 8.5)

    def out_collect(start):
        collect_lines(out_stage, start)
    chunked(out_collect)
    store_out(out_stage, out)
    drain(9.0)

    average, cross = stat_finish(2, stat2)
    column(4, average)
    column(5, cross)

    def hidden_back(start):
        at = pl.ds(start, shard)
        total = jnp.zeros((shard, LANES), F32)
        for h in range(height):
            value = cols[3, at, :] * (
                cols[10, at, :] * back[at, line(h)]
                - cols[4, at, :]
                - normed2[at, line(h)] * cols[5, at, :]
            )
            total = total + value
            rounded = value.astype(BF16)
            hgrad[at, line(h)] = rounded
            put(cot_slab, rounded.astype(F32), start, h + 1)
        cols[SUM_T, at, :] = total
    chunked(hidden_back)
    drain(10.3)
    halo_h = halo_edges(3, hgrad)
    time_sum = lane_sum(cols[SUM_T])
    now = 10.5
    for k in range(count, len(streams)):
        grad(k, hgrad, act_slab)
        if k >= count + LAG:
            core_step(k - LAG)
        now += 0.1 * -(-(streams[k][3] - streams[k][2]) // LANES)
        drain(now)
    core_step(len(streams) - 2)
    halo_finish(3, halo_h, cot_slab)
    core_step(len(streams) - 1)
    drain(now + 0.5)
    for begin in (0, half):
        back[:, begin : begin + half] = conv(
            lambda at: wturn1[:, at], cot_slab, begin, begin + half
        )
        drain(now + (1.8 if begin == 0 else 3.0))

    def first_slope(start):
        at = pl.ds(start, shard)
        sums = [jnp.zeros((shard, LANES), F32)] * 2
        for h in range(height):
            normed = normed1[at, line(h)]
            pre = cols[8, at, :] * normed + cols[9, at, :]
            q = 1.0 / (1.0 + jnp.exp(-pre))
            slope = back[at, line(h)] * (q * (1.0 + pre * (1.0 - q)))
            back[at, line(h)] = slope
            sums = [sums[0] + slope * normed, sums[1] + slope]
        cols[SUM_A, at, :] = sums[0]
        cols[SUM_B, at, :] = sums[1]
    chunked(first_slope)
    drain(now + 3.8)
    gain_cross1, bias_sum1 = lane_sum(cols[SUM_A]), lane_sum(cols[SUM_B])
    stat3 = stat_start(3, GAIN1 * bias_sum1, GAIN1 * gain_cross1)
    packed = jnp.zeros((channels, LANES), F32)
    for i, value in enumerate((time_sum, gain_cross1, bias_sum1, gain_cross2, bias_sum2)):
        packed = jnp.where(wide == i, value, packed)
    fill = jnp.zeros((tiny.shape[2] - channels, LANES), F32)
    tiny[row] = jnp.concatenate([packed, fill], axis=0).T[:8, :]
    tiny_rows = to_rows(tiny.at[row], tiny.at[row])
    drain(now + 6.0)

    drain(now + 7.0)
    average, cross = stat_finish(3, stat3)
    column(6, average)
    column(7, cross)

    for copy in tiny_rows:
        copy.wait_recv()
    total = tiny[0]
    for i in range(1, rows):
        total = total + tiny[i]
    tiny_x[0] = total
    first_hop = go(tiny_x.at[0], tiny_x.at[1], {"zero": mate})

    def input_back(start):
        at = pl.ds(start, shard)
        for h in range(height):
            value = cols[1, at, :] * (
                cols[8, at, :] * back[at, line(h)]
                - cols[6, at, :]
                - normed1[at, line(h)] * cols[7, at, :]
            )
            write_line(start, h, gs[at, line(h)].astype(F32) + value)
        collect_lines(gin_stage, start)
    chunked(input_back)
    store_out(gin_stage, gin)
    drain(now + 8.5)

    first_hop.wait_recv()
    tiny_x[2] = total + tiny_x[1]
    second_hop = go(tiny_x.at[2], tiny_x.at[3], {"zero": over})
    drain(now + 12.0)
    second_hop.wait_recv()
    pick = lax.broadcasted_iota(jnp.int32, total.shape, 0)
    small[...] = jnp.where(pick == 0, total, tiny_x[2] + tiny_x[3])
    drain(events[-3][0])
    for copy in pending:
        copy.wait_send()
    drain(1000.0)
    for copy in stores:
        copy.wait()


def deliver(
    out, gin, small, dw1, dw2, out_to, gin_to, time_to, norms_to, dw1_to, dw2_to,
    fields, grads, get, put,
):
    moves = []
    for i, (src, held, dst) in enumerate((
        (out, fields.at[0], out_to), (gin, fields.at[1], gin_to),
        (dw2, grads.at[1], dw2_to), (dw1, grads.at[0], dw1_to),
    )):
        first = pltpu.make_async_copy(src, held, get.at[i])
        first.start()
        moves.append((first, pltpu.make_async_copy(held, dst, put.at[i])))
    channels = time_to.shape[1]
    time_to[...] = small[0:1, 0:channels]
    norms_to[...] = small[1:5, 0:channels]
    for first, then in moves:
        first.wait()
        then.start()
    for _, then in moves:
        then.wait()


SECOND = (4 * LANES, 4 * LANES, 4 * LANES)
FIRST = (4 * LANES, 4 * LANES, 4 * LANES)
COMMON1, COMMON2 = 32, 32
START, RESTART, PACE, DELAY = 2.6, 13.0, 0.4, 1.8


def local(latents, time_shift, conv_first, conv_second, norm_gains, norm_biases, grad_output):
    _, channels, height, width = latents.shape
    cells = height * width
    shard, taps, _ = conv_first.shape
    rows = lax.axis_size("rows")
    blocks = channels // shard
    used = taps // 3 * channels
    band = -(-used // LANES) * LANES
    span = 3 * band
    units = span // LANES
    padded_cells = cells + 2 * LANES
    chain = BF16 if rows <= 8 else F32
    padded = -(-channels // LANES) * LANES
    vmem = pl.BlockSpec(memory_space=pltpu.VMEM)
    hbm = pl.BlockSpec(memory_space=pl.ANY)
    streams = sum(-(-used // width) for width in SECOND + FIRST)
    copies = 5 * (rows - 1) + 8 + 2 * 18 + streams * 5 + 2
    field = jax.ShapeDtypeStruct((channels, height, width), BF16)
    grads = jax.ShapeDtypeStruct((taps, shard, channels), F32)
    results = pl.pallas_call(
        block_kernel,
        out_shape=(field, field, jax.ShapeDtypeStruct((8, padded), F32), grads, grads),
        in_specs=[hbm, hbm, vmem, vmem, vmem, hbm, hbm],
        out_specs=(hbm, hbm, vmem, hbm, hbm),
        scratch_shapes=[
            pltpu.VMEM((channels, height, width), BF16),
            pltpu.VMEM((channels, height, width), BF16),
            pltpu.VMEM((taps, shard, channels), BF16),
            pltpu.VMEM((taps, shard, channels), BF16),
            pltpu.VMEM((NORM_GROUPS, channels), F32),
            pltpu.VMEM((channels, NORM_GROUPS), F32),
            pltpu.VMEM((used, padded_cells), BF16),
            pltpu.VMEM((used, padded_cells), BF16),
            pltpu.VMEM((used, padded_cells), BF16),
            pltpu.VMEM((blocks, shard, span), BF16),
            pltpu.VMEM((blocks, shard, span), BF16),
            pltpu.VMEM((channels, span), BF16),
            pltpu.VMEM((channels, span), BF16),
            pltpu.VMEM((channels, cells), BF16),
            pltpu.VMEM((channels, cells), BF16),
            pltpu.VMEM((channels, cells), BF16),
            pltpu.VMEM((channels, cells), F32),
            pltpu.VMEM((channels, cells), F32),
            pltpu.VMEM((channels, cells), F32),
            pltpu.VMEM((channels, cells), BF16),
            pltpu.VMEM((channels * height, LANES), F32),
            pltpu.VMEM((18, channels, LANES), F32),
            pltpu.VMEM((4, rows, NORM_GROUPS, LANES), F32),
            pltpu.VMEM((4, 2, channels, LANES), BF16),
            pltpu.VMEM((2, blocks, units, shard, LANES), BF16),
            pltpu.VMEM((2, 2, units, shard, LANES), BF16),
            pltpu.VMEM((2, units, shard, LANES), BF16),
            pltpu.VMEM((2, units, shard, LANES), BF16),
            pltpu.VMEM((2, units, shard, LANES), BF16),
            pltpu.VMEM((2, 2, units, shard, LANES), chain),
            pltpu.VMEM((2, 2, units, shard, LANES), chain),
            pltpu.VMEM((2, units, shard, LANES), F32),
            pltpu.VMEM((channels, height, LANES), BF16),
            pltpu.VMEM((channels, height, LANES), BF16),
            pltpu.VMEM((2, taps, shard, channels), F32),
            pltpu.VMEM((LANES, padded), F32),
            pltpu.VMEM((rows, 8, padded), F32),
            pltpu.VMEM((4, 8, padded), F32),
            pltpu.SemaphoreType.DMA((copies,)),
            pltpu.SemaphoreType.DMA((copies,)),
            pltpu.SemaphoreType.DMA((8,)),
            pltpu.SemaphoreType.DMA((4,)),
        ],
        compiler_params=pltpu.CompilerParams(
            collective_id=0, has_side_effects=True, vmem_limit_bytes=60 * 1024 * 1024
        ),
    )(
        latents.reshape(channels, height, width),
        grad_output.reshape(channels, height, width),
        norm_gains,
        norm_biases,
        time_shift,
        jnp.transpose(conv_first, (1, 0, 2)),
        jnp.transpose(conv_second, (1, 0, 2)),
    )
    out, gin, time_grad, norms, dw1, dw2 = pl.pallas_call(
        deliver,
        out_shape=(
            field,
            field,
            jax.ShapeDtypeStruct((1, channels), F32),
            jax.ShapeDtypeStruct((4, channels), F32),
            grads,
            grads,
        ),
        in_specs=[hbm, hbm, vmem, hbm, hbm],
        out_specs=(hbm, hbm, vmem, vmem, hbm, hbm),
        scratch_shapes=[
            pltpu.VMEM((2, channels, height, width), BF16),
            pltpu.VMEM((2, taps, shard, channels), F32),
            pltpu.SemaphoreType.DMA((4,)),
            pltpu.SemaphoreType.DMA((4,)),
        ],
    )(*results)
    return (
        out.reshape(latents.shape),
        gin.reshape(latents.shape),
        time_grad,
        jnp.transpose(dw1, (1, 0, 2)),
        jnp.transpose(dw2, (1, 0, 2)),
        norms,
    )


def solution(mesh):
    placed = (
        P(("groups", "zero"), None, "rows", None),
        P(("groups", "zero"), None),
        P("zero", None, None),
        P("zero", None, None),
        P(),
        P(),
        P(("groups", "zero"), None, "rows", None),
    )
    return jax.shard_map(
        local,
        mesh=mesh,
        in_specs=placed,
        out_specs=(
            P(("groups", "zero"), None, "rows", None),
            P(("groups", "zero"), None, "rows", None),
            P(("groups", "zero"), None),
            P(("groups", "zero"), None, None),
            P(("groups", "zero"), None, None),
            P("groups", None),
        ),
        check_vma=False,
    )
```
